128 devices in a mesh: tile: 16 (over x, z), depth: 8 (over y, core).
Axes of the slice: x: 4, y: 4, z: 4, core: 2. Of those that a mesh axis runs over, the one named last changes fastest.
Arguments:
- volume: float32 [512, 512, 1024], P('tile', 'depth')
- slab_place: int32 [8], replicated, may hold values from 0 to 7, each once
- control_index: int32 [8], replicated, may hold values from 0 to 255, as said below
- control_extinction: float32 [8], replicated, may hold values from 0.0001953125 to 0.01171875
- control_color: float32 [3, 8], replicated, may hold values from 0.2 to 1
Outputs:
- image: float32 [3, 512, 1024], P(None, 'tile', 'depth')
The draws below stay inside these ranges and needn't reach their ends.
Inputs may be any that keep to these rules, and one draw needn't show every extreme that they name: `slab_place`: each view position is given to exactly one slab. `control_index`: strictly increasing; the first is 0 and the last is 255.
All inputs are finite; a program needn't handle non-finite values.
Results may differ from the reference program's by a relative error of at most 0.0003.
Values sent between devices are 32-bit elements; how exact they have to be, the bound alone decides.
A program may use at most 128 MiB of HBM per device.

```python
import math
import jax
import jax.numpy as jnp
from jax import lax

ROWS_DEV = 32
SLAB = 64
COLS = 1024
CP = 8
TABLE = 256
NX = 512
NZ = 512
N_TILE = 16
N_DEPTH = 8


def draw_volume(key, part):
    row_ramp = jnp.arange(NX, dtype=jnp.float32)[:, None, None] / max(NX - 1, 1)
    depth_ramp = jnp.arange(NZ, dtype=jnp.float32)[None, :, None] / max(NZ - 1, 1)
    factor = 1.0 + row_ramp + depth_ramp
    noise = jax.random.normal(key, (NX, NZ, COLS), jnp.float32)
    return factor * noise


def draw_control_index(key, part):
    inner = jax.random.permutation(key, TABLE - 2)[:CP - 2] + 1
    inner = jnp.sort(inner.astype(jnp.int32))
    first = jnp.zeros((1,), jnp.int32)
    last = jnp.full((1,), TABLE - 1, jnp.int32)
    return jnp.concatenate([first, inner, last])


def setup_inputs(seed: int = 0) -> dict:
    arg_keys = jax.random.split(jax.random.key(seed), 6)
    volume = draw_volume(jax.random.fold_in(arg_keys[5], 71), 0)
    slab_place = jax.random.permutation(arg_keys[1], N_DEPTH).astype(jnp.int32)
    control_index = draw_control_index(jax.random.fold_in(arg_keys[5], 71), 0)
    control_extinction = jnp.clip(jnp.exp(jax.random.uniform(arg_keys[3], (CP,), jnp.float32, math.log(0.0001953125), math.log(0.01171875))), 0.0001953125, 0.01171875)
    control_color = jnp.clip(jax.random.uniform(arg_keys[4], (3, CP), jnp.float32, 0.2, 1.0), 0.2, 1.0)
    return dict(volume=volume, slab_place=slab_place, control_index=control_index, control_extinction=control_extinction, control_color=control_color)


def transfer(position, control_index, control_extinction, control_color):
    points = control_index.astype(jnp.float32)
    point_count = control_index.shape[0]
    extinct = jnp.zeros_like(position)
    emitted = [jnp.zeros_like(position) for channel in range(3)]
    for point in range(point_count):
        if point > 0:
            rising = (position - points[point - 1]) / (points[point] - points[point - 1])
        else:
            rising = jnp.ones_like(position)
        if point + 1 < point_count:
            falling = (points[point + 1] - position) / (points[point + 1] - points[point])
        else:
            falling = jnp.ones_like(position)
        hat_weight = jnp.maximum(0.0, jnp.minimum(rising, falling))
        extinct = extinct + hat_weight * control_extinction[point]
        emitted = [emitted[channel] + hat_weight * control_color[channel, point] for channel in range(3)]
    return (extinct, emitted)

def shade_slab(rows_padded, front_plane, back_plane, low_value, high_value, control_index, control_extinction, control_color):
    center = rows_padded[1:-1]
    grad_rows = 0.5 * (rows_padded[2:] - rows_padded[:-2])
    deepened = jnp.concatenate([front_plane[:, None], center, back_plane[:, None]], axis=1)
    grad_depth = 0.5 * (deepened[:, 2:] - deepened[:, :-2])
    widened = jnp.pad(center, ((0, 0), (0, 0), (1, 1)))
    grad_cols = 0.5 * (widened[:, :, 2:] - widened[:, :, :-2])
    facing = 0.48 * grad_rows + 0.6 * grad_depth + 0.64 * grad_cols
    shading = 0.3 + 0.7 * jnp.abs(facing) * lax.rsqrt(grad_rows * grad_rows + grad_depth * grad_depth + grad_cols * grad_cols + 1.0)
    position = (center - low_value) / (high_value - low_value + 1.0) * (TABLE - 1.0)
    extinct, emitted = transfer(position, control_index, control_extinction, control_color)
    opacity = 1.0 - jnp.exp(-extinct)
    plane_ids = jnp.arange(center.shape[1], dtype=jnp.int32)
    earlier_mask = (plane_ids[:, None] > plane_ids[None, :]).astype(jnp.float32)
    optical = jnp.einsum('zy,ryc->rzc', earlier_mask, extinct, precision=lax.Precision.HIGHEST)
    contrib = jnp.exp(-optical) * opacity * shading
    colors = jnp.stack([lax.optimization_barrier(jnp.sum(contrib * emitted[channel], axis=1)) for channel in range(3)], axis=0)
    transmit = jnp.exp(-lax.optimization_barrier(jnp.sum(extinct, axis=1)))
    return (colors, transmit)

def reference(volume, slab_place, control_index, control_extinction, control_color):
    high_value = jnp.max(volume)
    low_value = jnp.min(volume)
    slots = N_DEPTH
    positions = jnp.arange(slots, dtype=jnp.int32)
    inverse = lax.optimization_barrier(jnp.sum(jnp.where(slab_place[:, None] == positions[None, :], positions[:, None], 0), axis=0)).astype(jnp.int32)
    padded = jnp.pad(volume, ((1, 1), (0, 0), (0, 0)))

    def render_band(band):
        start = (band * ROWS_DEV).astype(jnp.int32)
        block = lax.dynamic_slice_in_dim(padded, start, ROWS_DEV + 2, 0)
        slabs = block.reshape(ROWS_DEV + 2, slots, SLAB, COLS)
        ordered = jnp.take(slabs, inverse, axis=1)
        zero_plane = jnp.zeros((ROWS_DEV, COLS), jnp.float32)
        image = jnp.zeros((3, ROWS_DEV, COLS), jnp.float32)
        carried = jnp.ones((ROWS_DEV, COLS), jnp.float32)
        for place_now in range(slots):
            front_plane = ordered[1:-1, place_now - 1, -1] if place_now > 0 else zero_plane
            back_plane = ordered[1:-1, place_now + 1, 0] if place_now + 1 < slots else zero_plane
            colors, transmit = shade_slab(ordered[:, place_now], front_plane, back_plane, low_value, high_value, control_index, control_extinction, control_color)
            image = image + carried[None] * colors
            carried = carried * transmit
        return image
    bands = lax.map(render_band, jnp.arange(N_TILE, dtype=jnp.int32))
    return jnp.transpose(bands, (1, 0, 2, 3)).reshape(3, NX, COLS)
```

```python
import functools

import jax
import jax.numpy as jnp
import numpy as np
from jax import lax
from jax.experimental import pallas as pl
from jax.experimental.pallas import tpu as pltpu
from jax.sharding import PartitionSpec as P

MESH = pl.DeviceIdType.MESH
TABLE = 256
LANES = 128
SUB = 8
PITCH = 8
KA, KB, KC = 0.48 / 0.64, 0.6 / 0.64, 0.7 * 0.64
BASE = 0.3 / KC
LOG2E = float(np.log2(np.e))
BIG = 3.0e38


def full(value):
    return jnp.full((SUB, LANES), value, jnp.float32)


def lookup(table, index):
    dims = lax.GatherDimensionNumbers(
        offset_dims=(),
        collapsed_slice_dims=(0,),
        start_index_map=(0,),
        operand_batching_dims=(1,),
        start_indices_batching_dims=(1,),
    )
    return lax.gather(
        table, index[..., None], dims, (1, 1), mode=lax.GatherScatterMode.PROMISE_IN_BOUNDS
    )


def shade(row_diff, plane_diff, col_diff):
    facing = (col_diff + KB * plane_diff) + KA * row_diff
    norm = (row_diff * row_diff + plane_diff * plane_diff) + (col_diff * col_diff + 1.0)
    return BASE + jnp.abs(facing) * lax.rsqrt(norm)


def col_diffs(tiles, lane):
    right = [pltpu.roll(x, 1, 1) for x in tiles]
    left = [pltpu.roll(x, LANES - 1, 1) for x in tiles]
    zero = jnp.zeros((SUB, LANES), jnp.float32)
    last = len(tiles) - 1
    out = []
    for c in range(len(tiles)):
        prev = jnp.where(lane == 0, right[c - 1] if c else zero, right[c])
        nxt = jnp.where(lane == LANES - 1, left[c + 1] if c < last else zero, left[c])
        out.append(nxt - prev)
    return out


def kernel(
    dims,
    volume,
    place_hbm,
    index_hbm,
    extinct_hbm,
    color_hbm,
    out,
    vol,
    shaded,
    face_in,
    face_out,
    face,
    part1,
    part2,
    packed,
    gathered,
    place,
    index,
    extinct,
    color,
    slots,
    param_sem,
    load_sem,
    halo_send,
    halo_recv,
    f1_send,
    f1_recv,
    f2_send,
    f2_recv,
    m1_send,
    m1_recv,
    m2_send,
    m2_recv,
    out_send,
    out_recv,
):
    tiles_n, slabs, rows, planes, cols = dims
    ct = cols // LANES
    blocks = rows // SUB
    me = lax.axis_index("depth")
    tile = lax.axis_index("tile")
    below = lax.rem(tile + 1, tiles_n)
    above = lax.rem(tile + tiles_n - 1, tiles_n)

    def depth_peer(j):
        return lax.rem(me + j, slabs)

    def tile_peer(j):
        return lax.rem(tile + j, tiles_n)

    params = [
        pltpu.make_async_copy(src, dst, param_sem.at[i])
        for i, (src, dst) in enumerate(
            ((place_hbm, place), (index_hbm, index), (extinct_hbm, extinct), (color_hbm, color))
        )
    ]
    for copy in params:
        copy.start()

    def columns(c):
        return pl.ds(pl.multiple_of(c * LANES, LANES), LANES)

    def load(c):
        return pltpu.make_async_copy(
            volume.at[:, :, columns(c)],
            vol.at[c, pl.ds(1, rows), pl.ds(0, planes), :],
            load_sem.at[c],
        )

    for c in range(ct):
        load(c).start()

    barrier = pltpu.get_barrier_semaphore()
    for j in range(1, slabs):
        pl.semaphore_signal(
            barrier, inc=1, device_id={"depth": depth_peer(j)}, device_id_type=MESH
        )
    for j in range(1, tiles_n):
        pl.semaphore_signal(barrier, inc=1, device_id={"tile": tile_peer(j)}, device_id_type=MESH)

    for copy in params:
        copy.wait()
    slots[0] = slabs
    slots[slabs + 1] = slabs
    for p in range(slabs):
        found = jnp.int32(0)
        for s in range(slabs):
            found = jnp.where(place[s] == p, jnp.int32(s), found)
        slots[p + 1] = lax.rem(me - found + slabs, slabs)
    zero = jnp.zeros((SUB, LANES), jnp.float32)
    for side in range(2):
        for b in range(blocks):
            face_in[slabs, side, pl.ds(b * SUB, SUB), :] = zero

    pl.semaphore_wait(barrier, slabs - 1 + tiles_n - 1)

    def halo(side, c):
        row = rows - 1 if side == 0 else 0
        return pltpu.make_async_remote_copy(
            src_ref=volume.at[row, :, columns(c)],
            dst_ref=vol.at[c, rows + 1 if side else 0, pl.ds(0, planes), :],
            send_sem=halo_send.at[side, c],
            recv_sem=halo_recv.at[side, c],
            device_id={"tile": above if side else below},
            device_id_type=MESH,
        )

    def face_first(j, side):
        owner = depth_peer(j)
        src = volume.at[
            :, side * (planes - 1), columns(owner)
        ]
        if j == 0:
            return pltpu.make_async_copy(src, face_in.at[0, side], f1_send.at[0, side])
        return pltpu.make_async_remote_copy(
            src_ref=src,
            dst_ref=face_in.at[j, side],
            send_sem=f1_send.at[j, side],
            recv_sem=f1_recv.at[j, side],
            device_id={"depth": owner},
            device_id_type=MESH,
        )

    def face_second(j):
        return pltpu.make_async_remote_copy(
            src_ref=face_out.at[j],
            dst_ref=face.at[me],
            send_sem=f2_send.at[j],
            recv_sem=f2_recv.at[j],
            device_id={"depth": depth_peer(j)},
            device_id_type=MESH,
        )

    for j in range(slabs):
        for side in range(2):
            face_first(j, side).start()

    @pl.when(tile < tiles_n - 1)
    def _():
        for c in range(ct):
            halo(0, c).start()

    @pl.when(tile > 0)
    def _():
        for c in range(ct):
            halo(1, c).start()

    pieces = planes // SUB

    def extremes_block(c, carry):
        load(c).wait()

        def step(r, carry):
            high, low = carry
            new_high, new_low = [], []
            for q in range(pieces):
                at = vol.at[c, r + 1, pl.ds(q * SUB, SUB), :]
                half = at[...] * 0.5
                at[...] = half
                new_high.append(jnp.maximum(high[q], half))
                new_low.append(jnp.minimum(low[q], half))
            return tuple(new_high), tuple(new_low)

        return lax.fori_loop(0, rows, step, carry, unroll=4)

    start = (tuple([full(-BIG)] * pieces), tuple([full(BIG)] * pieces))
    high, low = lax.fori_loop(0, ct, extremes_block, start)
    part1[0, 0:1, :] = jnp.max(functools.reduce(jnp.maximum, high), axis=0, keepdims=True)
    part1[0, 1:2, :] = -jnp.min(functools.reduce(jnp.minimum, low), axis=0, keepdims=True)

    def part_copy(stage, j):
        buf, send, recv = (part1, m1_send, m1_recv) if stage == 1 else (part2, m2_send, m2_recv)
        peer = {"depth": depth_peer(j)} if stage == 1 else {"tile": tile_peer(j)}
        return pltpu.make_async_remote_copy(
            src_ref=buf.at[0],
            dst_ref=buf.at[j],
            send_sem=send.at[j],
            recv_sem=recv.at[j],
            device_id=peer,
            device_id_type=MESH,
        )

    for j in range(1, slabs):
        part_copy(1, j).start()

    for j in range(slabs):
        for side in range(2):
            if j == 0:
                face_first(j, side).wait()
            else:
                face_first(j, side).wait_recv()
    for j in range(slabs):
        at = place[depth_peer(j)]
        front = slots[at]
        back = slots[at + 2]
        for b in range(blocks):
            rs = pl.ds(b * SUB, SUB)
            front_value = face_in[front, 1, rs, :] * 0.5
            back_value = face_in[back, 0, rs, :] * 0.5
            if j == 0:
                face[me, 0, rs, :] = front_value
                face[me, 1, rs, :] = back_value
            else:
                face_out[j, 0, rs, :] = front_value
                face_out[j, 1, rs, :] = back_value
        if j:
            face_second(j).start()

    pitch = planes + PITCH
    flat = vol.reshape(ct, (rows + 2) * pitch, LANES)

    def view(p, c, b, shift):
        return flat[c, pl.ds((b * SUB + 1 + shift) * pitch + p, SUB, stride=pitch), :]

    lane = lax.broadcasted_iota(jnp.int32, (SUB, LANES), 1)
    sub = lax.broadcasted_iota(jnp.int32, (SUB, LANES), 0)

    def shade_block(b):
        def step(i, carry):
            p = i + 1
            prev, here = carry[:ct], carry[ct:]
            nxt = tuple(view(p + 1, c, b, 0) for c in range(ct))
            diffs = col_diffs(here, lane)
            for c in range(ct):
                shaded[b, c, p] = shade(
                    view(p, c, b, 1) - view(p, c, b, -1), nxt[c] - prev[c], diffs[c]
                )
            return tuple(here) + nxt

        first = tuple(view(p, c, b, 0) for p in range(2) for c in range(ct))
        lax.fori_loop(0, planes - 2, step, first, unroll=31)

    def inner(i, _):
        shade_block(i + 1)
        return 0

    lax.fori_loop(0, 1, inner, 0)

    for j in range(1, slabs):
        part_copy(1, j).wait_recv()
    part2[0] = jnp.max(part1[...], axis=0)
    for j in range(1, tiles_n):
        part_copy(2, j).start()

    lax.fori_loop(1, blocks - 2, inner, 0)

    def halo_row(side, scale):
        def step(c, _):
            if scale:
                halo(side, c).wait_recv()
            for q in range(pieces):
                at = vol.at[c, rows + 1 if side else 0, pl.ds(q * SUB, SUB), :]
                at[...] = at[...] * 0.5 if scale else zero
            return 0

        lax.fori_loop(0, ct, step, 0)

    @pl.when(tile > 0)
    def _():
        halo_row(0, True)

    @pl.when(tile == 0)
    def _():
        halo_row(0, False)

    @pl.when(tile < tiles_n - 1)
    def _():
        halo_row(1, True)

    @pl.when(tile == tiles_n - 1)
    def _():
        halo_row(1, False)

    def outer(i, _):
        shade_block(i * (blocks - 1))
        return 0

    lax.fori_loop(0, 2, outer, 0)

    for j in range(1, slabs):
        face_second(j).wait_recv()

    def edge_planes(b, _):
        rs = pl.ds(pl.multiple_of(b * SUB, SUB), SUB)
        for side in range(2):
            p = side * (planes - 1)
            diffs = col_diffs([view(p, c, b, 0) for c in range(ct)], lane)
            for c in range(ct):
                other = face[c, side, rs, :]
                if side == 0:
                    plane_diff = view(1, c, b, 0) - other
                else:
                    plane_diff = other - view(planes - 2, c, b, 0)
                shaded[b, c, p] = shade(view(p, c, b, 1) - view(p, c, b, -1), plane_diff, diffs[c])
        return 0

    lax.fori_loop(0, blocks, edge_planes, 0)

    def by_segment(values):
        table = full(values[0])
        for s in range(1, len(values)):
            table = jnp.where(sub == s, values[s], table)
        return table

    knots = index.shape[0]
    points = [index[k].astype(jnp.float32) for k in range(knots)]
    lower = by_segment(points[:-1])
    upper = by_segment(points[1:])
    width = jnp.where(sub < knots - 1, upper - lower, 1.0)
    offsets, slopes = [], []
    for channel in range(4):
        scale = -LOG2E if channel == 0 else KC
        values = [
            extinct[k] if channel == 0 else color[channel - 1, k] for k in range(knots)
        ]
        begin, end = by_segment(values[:-1]), by_segment(values[1:])
        slope = (end - begin) / width
        offsets.append((begin - slope * lower) * scale)
        slopes.append(slope * scale)

    for j in range(1, tiles_n):
        part_copy(2, j).wait_recv()
    extremes = jnp.max(jnp.max(part2[...], axis=0), axis=1, keepdims=True)
    extremes = jnp.broadcast_to(extremes, (2, LANES))
    low_value = jnp.broadcast_to(-extremes[1:2, :], (SUB, LANES))
    span = jnp.broadcast_to(extremes[0:1, :] + extremes[1:2, :], (SUB, LANES)) + 0.5
    unit = span * (1.0 / (TABLE - 1.0))
    slopes = [slope * ((TABLE - 1.0) / span) for slope in slopes]
    bounds = [points[k] * unit for k in range(1, knots - 1)]
    odd = jnp.where(sub >= 6, BIG, jnp.where(sub >= 4, bounds[4], jnp.where(sub >= 2, bounds[2], bounds[0])))

    group = 2

    def render_block(b, _):
        def render_group(g, _):
            def step(p, carry):
                out_carry = []
                for k in range(group):
                    through, sums = carry[k]
                    c = g * group + k
                    dist = view(p, c, b, 0) - low_value
                    even = jnp.where(dist >= bounds[1], 2, 0)
                    even = jnp.where(dist >= bounds[3], 4, even)
                    even = jnp.where(dist >= bounds[5], 6, even)
                    segment = jnp.where(dist >= lookup(odd, even), even + 1, even)
                    offset = [lookup(t, segment) for t in offsets]
                    slope = [lookup(t, segment) for t in slopes]
                    rest = through * jnp.exp2(offset[0] + slope[0] * dist)
                    weight = (through - rest) * shaded[b, c, p]
                    sums = tuple(
                        sums[i] + weight * (offset[i + 1] + slope[i + 1] * dist) for i in range(3)
                    )
                    out_carry.append((rest, sums))
                return tuple(out_carry)

            begin = tuple((full(1.0), (full(0.0),) * 3) for _ in range(group))
            done = lax.fori_loop(0, planes, step, begin, unroll=16)
            for k in range(group):
                at = columns(g * group + k)
                for i in range(3):
                    packed[b, i, :, at] = done[k][1][i]
                packed[b, 3, :, at] = done[k][0]
            return 0

        lax.fori_loop(0, ct // group, render_group, 0)
        for j in range(1, slabs):
            result_copy(b, j).start()
        mine = columns(me)
        for i in range(4):
            gathered[b, 0, i] = packed[b, i, :, mine]
        return 0

    def result_copy(b, j):
        peer = depth_peer(j)
        return pltpu.make_async_remote_copy(
            src_ref=packed.at[b, :, :, columns(peer)],
            dst_ref=gathered.at[b, j],
            send_sem=out_send.at[b, j],
            recv_sem=out_recv.at[b, j],
            device_id={"depth": peer},
            device_id_type=MESH,
        )

    lax.fori_loop(0, blocks, render_block, 0)

    def arrive(b, _):
        for j in range(1, slabs):
            result_copy(b, j).wait_recv()
        return 0

    lax.fori_loop(0, blocks, arrive, 0)

    def composite(b, _):
        rs = pl.ds(pl.multiple_of(b * SUB, SUB), SUB)
        through = full(1.0)
        sums = [full(0.0)] * 3
        for p in range(slabs):
            slot = slots[p + 1]
            for i in range(3):
                sums[i] = sums[i] + through * gathered[b, slot, i]
            through = through * gathered[b, slot, 3]
        for i in range(3):
            out[i, rs, :] = sums[i]
        return 0

    lax.fori_loop(0, blocks, composite, 0)

    @pl.when(tile < tiles_n - 1)
    def _():
        for c in range(ct):
            halo(0, c).wait_send()

    @pl.when(tile > 0)
    def _():
        for c in range(ct):
            halo(1, c).wait_send()

    for j in range(1, slabs):
        for side in range(2):
            face_first(j, side).wait_send()
        face_second(j).wait_send()
        part_copy(1, j).wait_send()
    for j in range(1, tiles_n):
        part_copy(2, j).wait_send()

    def drain(b, _):
        for j in range(1, slabs):
            result_copy(b, j).wait_send()
        return 0

    lax.fori_loop(0, blocks, drain, 0)


def solution(mesh):
    tiles_n, slabs = mesh.shape["tile"], mesh.shape["depth"]

    def body(volume, slab_place, control_index, control_extinction, control_color):
        rows, planes, cols = volume.shape
        ct, blocks = cols // LANES, rows // SUB
        dims = (tiles_n, slabs, rows, planes, cols)
        f32, dma = jnp.float32, pltpu.SemaphoreType.DMA
        return pl.pallas_call(
            functools.partial(kernel, dims),
            out_shape=jax.ShapeDtypeStruct((3, rows, cols // slabs), f32),
            in_specs=[pl.BlockSpec(memory_space=pl.ANY)] * 5,
            out_specs=pl.BlockSpec(memory_space=pltpu.VMEM),
            scratch_shapes=[
                pltpu.VMEM((ct, rows + 2, planes + PITCH, LANES), f32),
                pltpu.VMEM((blocks, ct, planes, SUB, LANES), f32),
                pltpu.VMEM((slabs + 1, 2, rows, LANES), f32),
                pltpu.VMEM((slabs, 2, rows, LANES), f32),
                pltpu.VMEM((slabs, 2, rows, LANES), f32),
                pltpu.VMEM((slabs, 2, LANES), f32),
                pltpu.VMEM((tiles_n, 2, LANES), f32),
                pltpu.VMEM((blocks, 4, SUB, cols), f32),
                pltpu.VMEM((blocks, slabs, 4, SUB, LANES), f32),
                pltpu.SMEM(slab_place.shape, jnp.int32),
                pltpu.SMEM(control_index.shape, jnp.int32),
                pltpu.SMEM(control_extinction.shape, f32),
                pltpu.SMEM(control_color.shape, f32),
                pltpu.SMEM((slabs + 2,), jnp.int32),
                dma((4,)),
                dma((ct,)),
                dma((2, ct)),
                dma((2, ct)),
                dma((slabs, 2)),
                dma((slabs, 2)),
                dma((slabs,)),
                dma((slabs,)),
                dma((slabs,)),
                dma((slabs,)),
                dma((tiles_n,)),
                dma((tiles_n,)),
                dma((blocks, slabs)),
                dma((blocks, slabs)),
            ],
            compiler_params=pltpu.CompilerParams(
                collective_id=0, has_side_effects=True, vmem_limit_bytes=48 << 20
            ),
            name="render",
        )(volume, slab_place, control_index, control_extinction, control_color)

    placed = (P("tile", "depth", None), P(), P(), P(), P())
    return jax.shard_map(
        body, mesh=mesh, in_specs=placed, out_specs=P(None, "tile", "depth"), check_vma=False
    )
```

```python
import functools

import jax
import jax.numpy as jnp
import numpy as np
from jax import lax
from jax.experimental import pallas as pl
from jax.experimental.pallas import tpu as pltpu
from jax.sharding import PartitionSpec as P

MESH = pl.DeviceIdType.MESH
TABLE = 256
LANES = 128
SUB = 8
PITCH = 8
KA, KB, KC = 0.48 / 0.64, 0.6 / 0.64, 0.7 * 0.64
BASE = 0.3 / KC
LOG2E = float(np.log2(np.e))
BIG = 3.0e38


def full(value):
    return jnp.full((SUB, LANES), value, jnp.float32)


def lookup(table, index):
    dims = lax.GatherDimensionNumbers(
        offset_dims=(),
        collapsed_slice_dims=(0,),
        start_index_map=(0,),
        operand_batching_dims=(1,),
        start_indices_batching_dims=(1,),
    )
    return lax.gather(
        table, index[..., None], dims, (1, 1), mode=lax.GatherScatterMode.PROMISE_IN_BOUNDS
    )


def shade(row_diff, plane_diff, col_diff):
    facing = (col_diff + KB * plane_diff) + KA * row_diff
    norm = (row_diff * row_diff + plane_diff * plane_diff) + (col_diff * col_diff + 1.0)
    return BASE + jnp.abs(facing) * lax.rsqrt(norm)


def col_diffs(tiles, lane):
    right = [pltpu.roll(x, 1, 1) for x in tiles]
    left = [pltpu.roll(x, LANES - 1, 1) for x in tiles]
    zero = jnp.zeros((SUB, LANES), jnp.float32)
    last = len(tiles) - 1
    out = []
    for c in range(len(tiles)):
        prev = jnp.where(lane == 0, right[c - 1] if c else zero, right[c])
        nxt = jnp.where(lane == LANES - 1, left[c + 1] if c < last else zero, left[c])
        out.append(nxt - prev)
    return out


def kernel(
    dims,
    volume,
    place_hbm,
    index_hbm,
    extinct_hbm,
    color_hbm,
    out,
    vol,
    shaded,
    face_in,
    face_out,
    face,
    part1,
    part2,
    packed,
    gathered,
    place,
    index,
    extinct,
    color,
    slots,
    param_sem,
    load_sem,
    halo_send,
    halo_recv,
    f1_send,
    f1_recv,
    f2_send,
    f2_recv,
    m1_send,
    m1_recv,
    m2_send,
    m2_recv,
    out_send,
    out_recv,
    mate_send,
    mate_recv,
):
    tiles_n, slabs, rows, planes, cols = dims
    ct = cols // LANES
    blocks = rows // SUB
    me = lax.axis_index("depth")
    tile = lax.axis_index("tile")
    below = lax.rem(tile + 1, tiles_n)
    above = lax.rem(tile + tiles_n - 1, tiles_n)

    def depth_peer(j):
        return lax.rem(me + j, slabs)

    def tile_peer(j):
        return lax.rem(tile + j, tiles_n)

    params = [
        pltpu.make_async_copy(src, dst, param_sem.at[i])
        for i, (src, dst) in enumerate(
            ((place_hbm, place), (index_hbm, index), (extinct_hbm, extinct), (color_hbm, color))
        )
    ]
    def columns(c):
        return pl.ds(pl.multiple_of(c * LANES, LANES), LANES)

    def load(c):
        return pltpu.make_async_copy(
            volume.at[:, :, columns(c)],
            vol.at[c, pl.ds(1, rows), pl.ds(0, planes), :],
            load_sem.at[c],
        )

    for c in range(ct):
        load(c).start()
    for copy in params:
        copy.start()

    barrier = pltpu.get_barrier_semaphore()
    for j in range(1, slabs):
        pl.semaphore_signal(
            barrier, inc=1, device_id={"depth": depth_peer(j)}, device_id_type=MESH
        )
    for j in range(1, tiles_n):
        pl.semaphore_signal(barrier, inc=1, device_id={"tile": tile_peer(j)}, device_id_type=MESH)

    for copy in params:
        copy.wait()
    slots[0] = slabs
    slots[slabs + 1] = slabs
    for p in range(slabs):
        found = jnp.int32(0)
        for s in range(slabs):
            found = jnp.where(place[s] == p, jnp.int32(s), found)
        slots[p + 1] = found
    zero = jnp.zeros((SUB, LANES), jnp.float32)
    for side in range(2):
        for b in range(blocks):
            face_in[slabs, side, pl.ds(b * SUB, SUB), :] = zero

    pl.semaphore_wait(barrier, slabs - 1 + tiles_n - 1)

    def halo(side, c):
        row = rows - 1 if side == 0 else 0
        return pltpu.make_async_remote_copy(
            src_ref=volume.at[row, :, columns(c)],
            dst_ref=vol.at[c, rows + 1 if side else 0, pl.ds(0, planes), :],
            send_sem=halo_send.at[side, c],
            recv_sem=halo_recv.at[side, c],
            device_id={"tile": above if side else below},
            device_id_type=MESH,
        )

    def face_first(j, side):
        owner = depth_peer(j)
        src = volume.at[
            :, side * (planes - 1), columns(owner)
        ]
        if j == 0:
            return pltpu.make_async_copy(src, face_in.at[me, side], f1_send.at[0, side])
        return pltpu.make_async_remote_copy(
            src_ref=src,
            dst_ref=face_in.at[me, side],
            send_sem=f1_send.at[j, side],
            recv_sem=f1_recv.at[j, side],
            device_id={"depth": owner},
            device_id_type=MESH,
        )

    def face_second(j):
        return pltpu.make_async_remote_copy(
            src_ref=face_out.at[j],
            dst_ref=face.at[me],
            send_sem=f2_send.at[j],
            recv_sem=f2_recv.at[j],
            device_id={"depth": depth_peer(j)},
            device_id_type=MESH,
        )

    for j in range(slabs):
        for side in range(2):
            face_first(j, side).start()

    @pl.when(tile < tiles_n - 1)
    def _():
        for c in range(ct):
            halo(0, c).start()

    @pl.when(tile > 0)
    def _():
        for c in range(ct):
            halo(1, c).start()

    pieces = planes // SUB

    def extremes_block(c, carry):
        load(c).wait()

        def step(r, carry):
            high, low = carry
            new_high, new_low = [], []
            for q in range(pieces):
                at = vol.at[c, r + 1, pl.ds(q * SUB, SUB), :]
                half = at[...] * 0.5
                at[...] = half
                new_high.append(jnp.maximum(high[q], half))
                new_low.append(jnp.minimum(low[q], half))
            return tuple(new_high), tuple(new_low)

        return lax.fori_loop(0, rows, step, carry, unroll=4)

    start = (tuple([full(-BIG)] * pieces), tuple([full(BIG)] * pieces))
    high, low = lax.fori_loop(0, ct, extremes_block, start)
    part1[0, 0:1, :] = jnp.max(functools.reduce(jnp.maximum, high), axis=0, keepdims=True)
    part1[0, 1:2, :] = -jnp.min(functools.reduce(jnp.minimum, low), axis=0, keepdims=True)

    def part_copy(stage, j):
        buf, send, recv = (part1, m1_send, m1_recv) if stage == 1 else (part2, m2_send, m2_recv)
        peer = {"depth": depth_peer(j)} if stage == 1 else {"tile": tile_peer(j)}
        return pltpu.make_async_remote_copy(
            src_ref=buf.at[0],
            dst_ref=buf.at[j],
            send_sem=send.at[j],
            recv_sem=recv.at[j],
            device_id=peer,
            device_id_type=MESH,
        )

    for j in range(1, slabs):
        part_copy(1, j).start()

    pitch = planes + PITCH
    flat = vol.reshape(ct, (rows + 2) * pitch, LANES)

    def view(p, c, b, shift):
        return flat[c, pl.ds((b * SUB + 1 + shift) * pitch + p, SUB, stride=pitch), :]

    lane = lax.broadcasted_iota(jnp.int32, (SUB, LANES), 1)
    sub = lax.broadcasted_iota(jnp.int32, (SUB, LANES), 0)

    def shade_block(b):
        def step(i, carry):
            p = i + 1
            prev, here = carry[:ct], carry[ct:]
            nxt = tuple(view(p + 1, c, b, 0) for c in range(ct))
            diffs = col_diffs(here, lane)
            for c in range(ct):
                shaded[b, c, p] = shade(
                    view(p, c, b, 1) - view(p, c, b, -1), nxt[c] - prev[c], diffs[c]
                )
            return tuple(here) + nxt

        first = tuple(view(p, c, b, 0) for p in range(2) for c in range(ct))
        lax.fori_loop(0, planes - 2, step, first, unroll=31)

    def inner(i, _):
        shade_block(i + 1)
        return 0

    lax.fori_loop(0, 1, inner, 0)

    for j in range(slabs):
        for side in range(2):
            if j == 0:
                face_first(j, side).wait()
            else:
                face_first(j, side).wait_recv()
    for j in range(slabs):
        at = place[depth_peer(j)]
        front = slots[at]
        back = slots[at + 2]
        for b in range(blocks):
            rs = pl.ds(b * SUB, SUB)
            front_value = face_in[front, 1, rs, :] * 0.5
            back_value = face_in[back, 0, rs, :] * 0.5
            if j == 0:
                face[me, 0, rs, :] = front_value
                face[me, 1, rs, :] = back_value
            else:
                face_out[j, 0, rs, :] = front_value
                face_out[j, 1, rs, :] = back_value
        if j:
            face_second(j).start()

    lax.fori_loop(1, blocks - 2, inner, 0)

    for j in range(1, slabs):
        part_copy(1, j).wait_recv()
    part2[0] = jnp.max(part1[...], axis=0)
    for j in range(1, tiles_n):
        part_copy(2, j).start()

    def halo_row(side, scale):
        def step(c, _):
            if scale:
                halo(side, c).wait_recv()
            for q in range(pieces):
                at = vol.at[c, rows + 1 if side else 0, pl.ds(q * SUB, SUB), :]
                at[...] = at[...] * 0.5 if scale else zero
            return 0

        lax.fori_loop(0, ct, step, 0)

    @pl.when(tile > 0)
    def _():
        halo_row(0, True)

    @pl.when(tile == 0)
    def _():
        halo_row(0, False)

    @pl.when(tile < tiles_n - 1)
    def _():
        halo_row(1, True)

    @pl.when(tile == tiles_n - 1)
    def _():
        halo_row(1, False)

    def outer(i, _):
        shade_block(i * (blocks - 1))
        return 0

    lax.fori_loop(0, 2, outer, 0)

    for j in range(1, slabs):
        face_second(j).wait_recv()

    def edge_planes(b, _):
        rs = pl.ds(pl.multiple_of(b * SUB, SUB), SUB)
        for side in range(2):
            p = side * (planes - 1)
            diffs = col_diffs([view(p, c, b, 0) for c in range(ct)], lane)
            for c in range(ct):
                other = face[c, side, rs, :]
                if side == 0:
                    plane_diff = view(1, c, b, 0) - other
                else:
                    plane_diff = other - view(planes - 2, c, b, 0)
                shaded[b, c, p] = shade(view(p, c, b, 1) - view(p, c, b, -1), plane_diff, diffs[c])
        return 0

    lax.fori_loop(0, blocks, edge_planes, 0)

    def by_segment(values):
        table = full(values[0])
        for s in range(1, len(values)):
            table = jnp.where(sub == s, values[s], table)
        return table

    knots = index.shape[0]
    points = [index[k].astype(jnp.float32) for k in range(knots)]
    lower = by_segment(points[:-1])
    upper = by_segment(points[1:])
    width = jnp.where(sub < knots - 1, upper - lower, 1.0)
    offsets, slopes = [], []
    for channel in range(4):
        scale = -LOG2E if channel == 0 else KC
        values = [
            extinct[k] if channel == 0 else color[channel - 1, k] for k in range(knots)
        ]
        begin, end = by_segment(values[:-1]), by_segment(values[1:])
        slope = (end - begin) / width
        offsets.append((begin - slope * lower) * scale)
        slopes.append(slope * scale)

    for j in range(1, tiles_n):
        part_copy(2, j).wait_recv()
    extremes = jnp.max(jnp.max(part2[...], axis=0), axis=1, keepdims=True)
    extremes = jnp.broadcast_to(extremes, (2, LANES))
    low_value = jnp.broadcast_to(-extremes[1:2, :], (SUB, LANES))
    span = jnp.broadcast_to(extremes[0:1, :] + extremes[1:2, :], (SUB, LANES)) + 0.5
    unit = span * (1.0 / (TABLE - 1.0))
    slopes = [slope * ((TABLE - 1.0) / span) for slope in slopes]
    bounds = [points[k] * unit for k in range(1, knots - 1)]
    odd = jnp.where(sub >= 6, BIG, jnp.where(sub >= 4, bounds[4], jnp.where(sub >= 2, bounds[2], bounds[0])))

    cores = 2
    chips = slabs // cores
    chip = me // cores
    mate = me + 1 - 2 * lax.rem(me, cores)

    def render(first, b):
        def step(p, carry):
            out_carry = []
            for k in range(cores):
                through, sums = carry[k]
                dist = view(p, first + k, b, 0) - low_value
                even = jnp.where(dist >= bounds[1], 2, 0)
                even = jnp.where(dist >= bounds[3], 4, even)
                even = jnp.where(dist >= bounds[5], 6, even)
                segment = jnp.where(dist >= lookup(odd, even), even + 1, even)
                offset = [lookup(t, segment) for t in offsets]
                slope = [lookup(t, segment) for t in slopes]
                rest = through * jnp.exp2(offset[0] + slope[0] * dist)
                weight = (through - rest) * shaded[b, first + k, p]
                sums = tuple(
                    sums[i] + weight * (offset[i + 1] + slope[i + 1] * dist) for i in range(3)
                )
                out_carry.append((rest, sums))
            return tuple(out_carry)

        begin = tuple((full(1.0), (full(0.0),) * 3) for _ in range(cores))
        done = lax.fori_loop(0, planes, step, begin, unroll=16)
        for k in range(cores):
            for i in range(3):
                packed[first + k, b, i] = done[k][1][i]
            packed[first + k, b, 3] = done[k][0]

    def result_copy(owner):
        return pltpu.make_async_remote_copy(
            src_ref=packed.at[owner],
            dst_ref=gathered.at[me],
            send_sem=out_send.at[owner],
            recv_sem=out_recv.at[me],
            device_id={"depth": owner},
            device_id_type=MESH,
        )

    def mate_copy(b):
        return pltpu.make_async_remote_copy(
            src_ref=packed.at[mate, b],
            dst_ref=gathered.at[me, b],
            send_sem=mate_send.at[b],
            recv_sem=mate_recv.at[b],
            device_id={"depth": mate},
            device_id_type=MESH,
        )

    def away(i, _):
        first = cores * lax.rem(chip + 2 + (3 * i * i - 5 * i) // 2, chips)

        def block(b, _):
            render(first, b)
            return 0

        lax.fori_loop(0, blocks, block, 0)
        for k in range(cores):
            result_copy(first + k).start()
        return 0

    lax.fori_loop(0, chips - 1, away, 0)

    def home(b, _):
        render(chip * cores, b)
        mate_copy(b).start()
        for i in range(4):
            gathered[me, b, i] = packed[me, b, i]
        return 0

    lax.fori_loop(0, blocks, home, 0)

    @pl.when(tile < tiles_n - 1)
    def _():
        for c in range(ct):
            halo(0, c).wait_send()

    @pl.when(tile > 0)
    def _():
        for c in range(ct):
            halo(1, c).wait_send()

    for j in range(1, slabs):
        for side in range(2):
            face_first(j, side).wait_send()
        face_second(j).wait_send()
        part_copy(1, j).wait_send()
    for j in range(1, tiles_n):
        part_copy(2, j).wait_send()

    def away_copy(i):
        return result_copy(lax.rem(cores * (chip + i // cores) + i % cores, slabs))

    for i in range(cores, slabs):
        away_copy(i).wait_send()
    for i in range(cores, slabs):
        sender = lax.rem(cores * (chip + i // cores) + i % cores, slabs)
        pltpu.make_async_remote_copy(
            src_ref=packed.at[sender],
            dst_ref=gathered.at[sender],
            send_sem=out_send.at[sender],
            recv_sem=out_recv.at[sender],
            device_id={"depth": sender},
            device_id_type=MESH,
        ).wait_recv()
    for b in range(blocks):
        mate_copy(b).wait_send()
    for b in range(blocks):
        pltpu.make_async_remote_copy(
            src_ref=packed.at[mate, b],
            dst_ref=gathered.at[mate, b],
            send_sem=mate_send.at[b],
            recv_sem=mate_recv.at[b],
            device_id={"depth": mate},
            device_id_type=MESH,
        ).wait_recv()

    def composite(b, _):
        rs = pl.ds(pl.multiple_of(b * SUB, SUB), SUB)
        through = full(1.0)
        sums = [full(0.0)] * 3
        for p in range(slabs):
            slot = slots[p + 1]
            for i in range(3):
                sums[i] = sums[i] + through * gathered[slot, b, i]
            through = through * gathered[slot, b, 3]
        for i in range(3):
            out[i, rs, :] = sums[i]
        return 0

    lax.fori_loop(0, blocks, composite, 0)


def solution(mesh):
    tiles_n, slabs = mesh.shape["tile"], mesh.shape["depth"]

    def body(volume, slab_place, control_index, control_extinction, control_color):
        rows, planes, cols = volume.shape
        ct, blocks = cols // LANES, rows // SUB
        dims = (tiles_n, slabs, rows, planes, cols)
        f32, dma = jnp.float32, pltpu.SemaphoreType.DMA
        return pl.pallas_call(
            functools.partial(kernel, dims),
            out_shape=jax.ShapeDtypeStruct((3, rows, cols // slabs), f32),
            in_specs=[pl.BlockSpec(memory_space=pltpu.HBM)] * 5,
            out_specs=pl.BlockSpec(memory_space=pltpu.VMEM),
            scratch_shapes=[
                pltpu.VMEM((ct, rows + 2, planes + PITCH, LANES), f32),
                pltpu.VMEM((blocks, ct, planes, SUB, LANES), f32),
                pltpu.VMEM((slabs + 1, 2, rows, LANES), f32),
                pltpu.VMEM((slabs, 2, rows, LANES), f32),
                pltpu.VMEM((slabs, 2, rows, LANES), f32),
                pltpu.VMEM((slabs, 2, LANES), f32),
                pltpu.VMEM((tiles_n, 2, LANES), f32),
                pltpu.VMEM((slabs, blocks, 4, SUB, LANES), f32),
                pltpu.VMEM((slabs, blocks, 4, SUB, LANES), f32),
                pltpu.SMEM(slab_place.shape, jnp.int32),
                pltpu.SMEM(control_index.shape, jnp.int32),
                pltpu.SMEM(control_extinction.shape, f32),
                pltpu.SMEM(control_color.shape, f32),
                pltpu.SMEM((slabs + 2,), jnp.int32),
                dma((4,)),
                dma((ct,)),
                dma((2, ct)),
                dma((2, ct)),
                dma((slabs, 2)),
                dma((slabs, 2)),
                dma((slabs,)),
                dma((slabs,)),
                dma((slabs,)),
                dma((slabs,)),
                dma((tiles_n,)),
                dma((tiles_n,)),
                dma((slabs,)),
                dma((slabs,)),
                dma((blocks,)),
                dma((blocks,)),
            ],
            compiler_params=pltpu.CompilerParams(
                collective_id=0, has_side_effects=True, vmem_limit_bytes=63 << 20
            ),
            name="render",
        )(volume, slab_place, control_index, control_extinction, control_color)

    placed = (P("tile", "depth", None), P(), P(), P(), P())
    return jax.shard_map(
        body, mesh=mesh, in_specs=placed, out_specs=P(None, "tile", "depth"), check_vma=False
    )
```

```python
import functools

import jax
import jax.numpy as jnp
import numpy as np
from jax import lax
from jax.experimental import pallas as pl
from jax.experimental.pallas import tpu as pltpu
from jax.sharding import PartitionSpec as P

MESH = pl.DeviceIdType.MESH
TABLE = 256
LANES = 128
SUB = 8
PITCH = 8
KA, KB, KC = 0.48 / 0.64, 0.6 / 0.64, 0.7 * 0.64
BASE = 0.3 / KC
LOG2E = float(np.log2(np.e))
BIG = 3.0e38


def full(value):
    return jnp.full((SUB, LANES), value, jnp.float32)


def lookup(table, index):
    dims = lax.GatherDimensionNumbers(
        offset_dims=(),
        collapsed_slice_dims=(0,),
        start_index_map=(0,),
        operand_batching_dims=(1,),
        start_indices_batching_dims=(1,),
    )
    return lax.gather(
        table, index[..., None], dims, (1, 1), mode=lax.GatherScatterMode.PROMISE_IN_BOUNDS
    )


def shade(row_diff, plane_diff, col_diff):
    facing = (col_diff + KB * plane_diff) + KA * row_diff
    norm = (row_diff * row_diff + plane_diff * plane_diff) + (col_diff * col_diff + 1.0)
    return BASE + jnp.abs(facing) * lax.rsqrt(norm)


def col_diffs(tiles, before, after, lane):
    right = [None if x is None else pltpu.roll(x, 1, 1) for x in (before, *tiles)]
    left = [None if x is None else pltpu.roll(x, LANES - 1, 1) for x in (*tiles, after)]
    right = [jnp.zeros_like(tiles[0]) if x is None else x for x in right]
    left = [jnp.zeros_like(tiles[0]) if x is None else x for x in left]
    return [
        jnp.where(lane == LANES - 1, left[k + 1], left[k])
        - jnp.where(lane == 0, right[k], right[k + 1])
        for k in range(len(tiles))
    ]


def kernel(
    dims,
    volume,
    place_hbm,
    index_hbm,
    extinct_hbm,
    color_hbm,
    out,
    vol,
    shaded,
    face_in,
    face_out,
    face,
    part1,
    part2,
    packed,
    gathered,
    place,
    index,
    extinct,
    color,
    slots,
    param_sem,
    load_sem,
    halo_send,
    halo_recv,
    f1_send,
    f1_recv,
    f2_send,
    f2_recv,
    m1_send,
    m1_recv,
    m2_send,
    m2_recv,
    out_send,
    out_recv,
):
    tiles_n, slabs, rows, planes, cols = dims
    ct = cols // LANES
    blocks = rows // SUB
    me = lax.axis_index("depth")
    tile = lax.axis_index("tile")
    below = lax.rem(tile + 1, tiles_n)
    above = lax.rem(tile + tiles_n - 1, tiles_n)

    def depth_peer(j):
        return lax.rem(me + j, slabs)

    def tile_peer(j):
        return lax.rem(tile + j, tiles_n)

    params = [
        pltpu.make_async_copy(src, dst, param_sem.at[i])
        for i, (src, dst) in enumerate(
            ((place_hbm, place), (index_hbm, index), (extinct_hbm, extinct), (color_hbm, color))
        )
    ]
    def columns(c):
        return pl.ds(pl.multiple_of(c * LANES, LANES), LANES)

    def load(c):
        return pltpu.make_async_copy(
            volume.at[:, :, columns(c)],
            vol.at[c, pl.ds(1, rows), pl.ds(0, planes), :],
            load_sem.at[c],
        )

    for c in range(ct):
        load(c).start()
    for copy in params:
        copy.start()

    barrier = pltpu.get_barrier_semaphore()
    for j in range(1, slabs):
        pl.semaphore_signal(
            barrier, inc=1, device_id={"depth": depth_peer(j)}, device_id_type=MESH
        )
    for j in range(1, tiles_n):
        pl.semaphore_signal(barrier, inc=1, device_id={"tile": tile_peer(j)}, device_id_type=MESH)

    for copy in params:
        copy.wait()
    slots[0] = slabs
    slots[slabs + 1] = slabs
    for p in range(slabs):
        found = jnp.int32(0)
        for s in range(slabs):
            found = jnp.where(place[s] == p, jnp.int32(s), found)
        slots[p + 1] = found
    zero = jnp.zeros((SUB, LANES), jnp.float32)
    for side in range(2):
        for b in range(blocks):
            face_in[slabs, side, pl.ds(b * SUB, SUB), :] = zero

    pl.semaphore_wait(barrier, slabs - 1 + tiles_n - 1)

    def halo(side, c):
        row = rows - 1 if side == 0 else 0
        return pltpu.make_async_remote_copy(
            src_ref=volume.at[row, :, columns(c)],
            dst_ref=vol.at[c, rows + 1 if side else 0, pl.ds(0, planes), :],
            send_sem=halo_send.at[side, c],
            recv_sem=halo_recv.at[side, c],
            device_id={"tile": above if side else below},
            device_id_type=MESH,
        )

    def face_first(j, side):
        owner = depth_peer(j)
        src = volume.at[
            :, side * (planes - 1), columns(owner)
        ]
        if j == 0:
            return pltpu.make_async_copy(src, face_in.at[me, side], f1_send.at[0, side])
        return pltpu.make_async_remote_copy(
            src_ref=src,
            dst_ref=face_in.at[me, side],
            send_sem=f1_send.at[j, side],
            recv_sem=f1_recv.at[j, side],
            device_id={"depth": owner},
            device_id_type=MESH,
        )

    def face_second(j):
        return pltpu.make_async_remote_copy(
            src_ref=face_out.at[j],
            dst_ref=face.at[me],
            send_sem=f2_send.at[j],
            recv_sem=f2_recv.at[j],
            device_id={"depth": depth_peer(j)},
            device_id_type=MESH,
        )

    for j in range(slabs):
        for side in range(2):
            face_first(j, side).start()

    @pl.when(tile < tiles_n - 1)
    def _():
        for c in range(ct):
            halo(0, c).start()

    @pl.when(tile > 0)
    def _():
        for c in range(ct):
            halo(1, c).start()

    pitch = planes + PITCH
    flat = vol.reshape(ct, (rows + 2) * pitch, LANES)

    def view(p, c, b, shift):
        return flat[c, pl.ds((b * SUB + 1 + shift) * pitch + p, SUB, stride=pitch), :]

    lane = lax.broadcasted_iota(jnp.int32, (SUB, LANES), 1)
    sub = lax.broadcasted_iota(jnp.int32, (SUB, LANES), 0)

    run = 2

    def shade_run(first, b):
        tiles = range(first, first + run)

        def step(i, carry):
            p = i + 1
            prev, here = carry[:run], carry[run:]
            nxt = tuple(view(p + 1, c, b, 0) for c in tiles)
            before = view(p, first - 1, b, 0) if first else None
            after = view(p, first + run, b, 0) if first + run < ct else None
            diffs = col_diffs(here, before, after, lane)
            for k, c in enumerate(tiles):
                shaded[b, c, p] = shade(
                    view(p, c, b, 1) - view(p, c, b, -1), nxt[k] - prev[k], diffs[k]
                )
            return tuple(here) + nxt

        first_two = tuple(view(p, c, b, 0) for p in range(2) for c in tiles)
        lax.fori_loop(0, planes - 2, step, first_two, unroll=31)

    def shade_inner(first):
        def block(b, _):
            shade_run(first, b)
            return 0

        lax.fori_loop(1, blocks - 1, block, 0)

    pieces = planes // SUB

    def extremes_block(c, carry):
        load(c).wait()

        def step(r, carry):
            high, low = carry
            new_high, new_low = [], []
            for q in range(pieces):
                at = vol.at[c, r + 1, pl.ds(q * SUB, SUB), :]
                half = at[...] * 0.5
                at[...] = half
                new_high.append(jnp.maximum(high[q], half))
                new_low.append(jnp.minimum(low[q], half))
            return tuple(new_high), tuple(new_low)

        return lax.fori_loop(0, rows, step, carry, unroll=4)

    start = (tuple([full(-BIG)] * pieces), tuple([full(BIG)] * pieces))
    extremes = lax.fori_loop(0, run + 1, extremes_block, start)
    shade_inner(0)
    extremes = lax.fori_loop(run + 1, 2 * run + 1, extremes_block, extremes)
    shade_inner(run)
    high, low = lax.fori_loop(2 * run + 1, ct, extremes_block, extremes)
    part1[0, 0:1, :] = jnp.max(functools.reduce(jnp.maximum, high), axis=0, keepdims=True)
    part1[0, 1:2, :] = -jnp.min(functools.reduce(jnp.minimum, low), axis=0, keepdims=True)

    def part_copy(stage, j):
        buf, send, recv = (part1, m1_send, m1_recv) if stage == 1 else (part2, m2_send, m2_recv)
        peer = {"depth": depth_peer(j)} if stage == 1 else {"tile": tile_peer(j)}
        return pltpu.make_async_remote_copy(
            src_ref=buf.at[0],
            dst_ref=buf.at[j],
            send_sem=send.at[j],
            recv_sem=recv.at[j],
            device_id=peer,
            device_id_type=MESH,
        )

    for j in range(1, slabs):
        part_copy(1, j).start()

    shade_inner(2 * run)

    for j in range(slabs):
        for side in range(2):
            if j == 0:
                face_first(j, side).wait()
            else:
                face_first(j, side).wait_recv()
    for j in range(slabs):
        at = place[depth_peer(j)]
        front = slots[at]
        back = slots[at + 2]
        for b in range(blocks):
            rs = pl.ds(b * SUB, SUB)
            front_value = face_in[front, 1, rs, :] * 0.5
            back_value = face_in[back, 0, rs, :] * 0.5
            if j == 0:
                face[me, 0, rs, :] = front_value
                face[me, 1, rs, :] = back_value
            else:
                face_out[j, 0, rs, :] = front_value
                face_out[j, 1, rs, :] = back_value
        if j:
            face_second(j).start()

    shade_inner(3 * run)

    for j in range(1, slabs):
        part_copy(1, j).wait_recv()
    part2[0] = jnp.max(part1[...], axis=0)
    for j in range(1, tiles_n):
        part_copy(2, j).start()

    def halo_row(side, scale):
        def step(c, _):
            if scale:
                halo(side, c).wait_recv()
            for q in range(pieces):
                at = vol.at[c, rows + 1 if side else 0, pl.ds(q * SUB, SUB), :]
                at[...] = at[...] * 0.5 if scale else zero
            return 0

        lax.fori_loop(0, ct, step, 0)

    @pl.when(tile > 0)
    def _():
        halo_row(0, True)

    @pl.when(tile == 0)
    def _():
        halo_row(0, False)

    @pl.when(tile < tiles_n - 1)
    def _():
        halo_row(1, True)

    @pl.when(tile == tiles_n - 1)
    def _():
        halo_row(1, False)

    def outer(i, _):
        for first in range(0, ct, run):
            shade_run(first, i * (blocks - 1))
        return 0

    lax.fori_loop(0, 2, outer, 0)

    for j in range(1, slabs):
        face_second(j).wait_recv()

    def edge_planes(b, _):
        rs = pl.ds(pl.multiple_of(b * SUB, SUB), SUB)
        for side in range(2):
            p = side * (planes - 1)
            diffs = col_diffs([view(p, c, b, 0) for c in range(ct)], None, None, lane)
            for c in range(ct):
                other = face[c, side, rs, :]
                if side == 0:
                    plane_diff = view(1, c, b, 0) - other
                else:
                    plane_diff = other - view(planes - 2, c, b, 0)
                shaded[b, c, p] = shade(view(p, c, b, 1) - view(p, c, b, -1), plane_diff, diffs[c])
        return 0

    lax.fori_loop(0, blocks, edge_planes, 0)

    def by_segment(values):
        table = full(values[0])
        for s in range(1, len(values)):
            table = jnp.where(sub == s, values[s], table)
        return table

    knots = index.shape[0]
    points = [index[k].astype(jnp.float32) for k in range(knots)]
    lower = by_segment(points[:-1])
    upper = by_segment(points[1:])
    width = jnp.where(sub < knots - 1, upper - lower, 1.0)
    offsets, slopes = [], []
    for channel in range(4):
        scale = -LOG2E if channel == 0 else KC
        values = [
            extinct[k] if channel == 0 else color[channel - 1, k] for k in range(knots)
        ]
        begin, end = by_segment(values[:-1]), by_segment(values[1:])
        slope = (end - begin) / width
        offsets.append((begin - slope * lower) * scale)
        slopes.append(slope * scale)

    for j in range(1, tiles_n):
        part_copy(2, j).wait_recv()
    extremes = jnp.max(jnp.max(part2[...], axis=0), axis=1, keepdims=True)
    extremes = jnp.broadcast_to(extremes, (2, LANES))
    low_value = jnp.broadcast_to(-extremes[1:2, :], (SUB, LANES))
    span = jnp.broadcast_to(extremes[0:1, :] + extremes[1:2, :], (SUB, LANES)) + 0.5
    unit = span * (1.0 / (TABLE - 1.0))
    slopes = [slope * ((TABLE - 1.0) / span) for slope in slopes]
    bounds = [points[k] * unit for k in range(1, knots - 1)]
    odd = jnp.where(sub >= 6, BIG, jnp.where(sub >= 4, bounds[4], jnp.where(sub >= 2, bounds[2], bounds[0])))

    cores = 2
    chips = slabs // cores
    chip = me // cores
    mate = me + 1 - 2 * lax.rem(me, cores)
    pair = 2

    def render(owner, result):
        def rows_pair(i, _):
            def step(p, carry):
                out_carry = []
                for k in range(pair):
                    b = i * pair + k
                    through, sums = carry[k]
                    dist = view(p, owner, b, 0) - low_value
                    even = jnp.where(dist >= bounds[1], 2, 0)
                    even = jnp.where(dist >= bounds[3], 4, even)
                    even = jnp.where(dist >= bounds[5], 6, even)
                    segment = jnp.where(dist >= lookup(odd, even), even + 1, even)
                    offset = [lookup(t, segment) for t in offsets]
                    slope = [lookup(t, segment) for t in slopes]
                    rest = through * jnp.exp2(offset[0] + slope[0] * dist)
                    weight = (through - rest) * shaded[b, owner, p]
                    sums = tuple(
                        sums[n] + weight * (offset[n + 1] + slope[n + 1] * dist)
                        for n in range(3)
                    )
                    out_carry.append((rest, sums))
                return tuple(out_carry)

            begin = tuple((full(1.0), (full(0.0),) * 3) for _ in range(pair))
            done = lax.fori_loop(0, planes, step, begin, unroll=32)
            for k in range(pair):
                for n in range(3):
                    result[owner, i * pair + k, n] = done[k][1][n]
                result[owner, i * pair + k, 3] = done[k][0]
            return 0

        lax.fori_loop(0, blocks // pair, rows_pair, 0)

    def result_copy(owner, sender):
        return pltpu.make_async_remote_copy(
            src_ref=packed.at[owner],
            dst_ref=gathered.at[sender],
            send_sem=out_send.at[owner],
            recv_sem=out_recv.at[sender],
            device_id={"depth": owner},
            device_id_type=MESH,
        )

    def away(i, _):
        n = i // cores
        owner = cores * lax.rem(chip + 2 + (3 * n * n - 5 * n) // 2, chips) + i % cores
        render(owner, packed)
        result_copy(owner, me).start()
        return 0

    lax.fori_loop(0, slabs - cores, away, 0)
    render(mate, packed)
    result_copy(mate, me).start()
    render(me, gathered)

    @pl.when(tile < tiles_n - 1)
    def _():
        for c in range(ct):
            halo(0, c).wait_send()

    @pl.when(tile > 0)
    def _():
        for c in range(ct):
            halo(1, c).wait_send()

    for j in range(1, slabs):
        for side in range(2):
            face_first(j, side).wait_send()
        face_second(j).wait_send()
        part_copy(1, j).wait_send()
    for j in range(1, tiles_n):
        part_copy(2, j).wait_send()

    for j in range(1, slabs):
        result_copy(depth_peer(j), me).wait_send()
    for j in range(1, slabs):
        result_copy(depth_peer(j), depth_peer(j)).wait_recv()

    def composite(b, _):
        rs = pl.ds(pl.multiple_of(b * SUB, SUB), SUB)
        through = full(1.0)
        sums = [full(0.0)] * 3
        for p in range(slabs):
            slot = slots[p + 1]
            for i in range(3):
                sums[i] = sums[i] + through * gathered[slot, b, i]
            through = through * gathered[slot, b, 3]
        for i in range(3):
            out[i, rs, :] = sums[i]
        return 0

    lax.fori_loop(0, blocks, composite, 0)


def solution(mesh):
    tiles_n, slabs = mesh.shape["tile"], mesh.shape["depth"]

    def body(volume, slab_place, control_index, control_extinction, control_color):
        rows, planes, cols = volume.shape
        ct, blocks = cols // LANES, rows // SUB
        dims = (tiles_n, slabs, rows, planes, cols)
        f32, dma = jnp.float32, pltpu.SemaphoreType.DMA
        return pl.pallas_call(
            functools.partial(kernel, dims),
            out_shape=jax.ShapeDtypeStruct((3, rows, cols // slabs), f32),
            in_specs=[pl.BlockSpec(memory_space=pltpu.HBM)] * 5,
            out_specs=pl.BlockSpec(memory_space=pltpu.VMEM),
            scratch_shapes=[
                pltpu.VMEM((ct, rows + 2, planes + PITCH, LANES), f32),
                pltpu.VMEM((blocks, ct, planes, SUB, LANES), f32),
                pltpu.VMEM((slabs + 1, 2, rows, LANES), f32),
                pltpu.VMEM((slabs, 2, rows, LANES), f32),
                pltpu.VMEM((slabs, 2, rows, LANES), f32),
                pltpu.VMEM((slabs, 2, LANES), f32),
                pltpu.VMEM((tiles_n, 2, LANES), f32),
                pltpu.VMEM((slabs, blocks, 4, SUB, LANES), f32),
                pltpu.VMEM((slabs, blocks, 4, SUB, LANES), f32),
                pltpu.SMEM(slab_place.shape, jnp.int32),
                pltpu.SMEM(control_index.shape, jnp.int32),
                pltpu.SMEM(control_extinction.shape, f32),
                pltpu.SMEM(control_color.shape, f32),
                pltpu.SMEM((slabs + 2,), jnp.int32),
                dma((4,)),
                dma((ct,)),
                dma((2, ct)),
                dma((2, ct)),
                dma((slabs, 2)),
                dma((slabs, 2)),
                dma((slabs,)),
                dma((slabs,)),
                dma((slabs,)),
                dma((slabs,)),
                dma((tiles_n,)),
                dma((tiles_n,)),
                dma((slabs,)),
                dma((slabs,)),
            ],
            compiler_params=pltpu.CompilerParams(
                collective_id=0, has_side_effects=True, vmem_limit_bytes=48 << 20
            ),
            name="render",
        )(
            volume,
            *(
                pltpu.with_memory_space_constraint(x, pltpu.HBM)
                for x in (slab_place, control_index, control_extinction, control_color)
            ),
        )

    placed = (P("tile", "depth", None), P(), P(), P(), P())
    return jax.shard_map(
        body, mesh=mesh, in_specs=placed, out_specs=P(None, "tile", "depth"), check_vma=False
    )
```

```python
import functools

import jax
import jax.numpy as jnp
import numpy as np
from jax import lax
from jax.experimental import pallas as pl
from jax.experimental.pallas import tpu as pltpu
from jax.sharding import PartitionSpec as P

MESH = pl.DeviceIdType.MESH
TABLE = 256
LANES = 128
SUB = 8
KA, KB, KC = 0.48 / 0.64, 0.6 / 0.64, 0.7 * 0.64
BASE = 0.3 / KC
LOG2E = float(np.log2(np.e))
BIG = 3.0e38


def full(value):
    return jnp.full((SUB, LANES), value, jnp.float32)


def lookup(table, index):
    dims = lax.GatherDimensionNumbers(
        offset_dims=(),
        collapsed_slice_dims=(0,),
        start_index_map=(0,),
        operand_batching_dims=(1,),
        start_indices_batching_dims=(1,),
    )
    return lax.gather(
        table, index[..., None], dims, (1, 1), mode=lax.GatherScatterMode.PROMISE_IN_BOUNDS
    )


def shade(row_diff, plane_diff, col_diff):
    facing = (col_diff + KB * plane_diff) + KA * row_diff
    norm = (row_diff * row_diff + plane_diff * plane_diff) + (col_diff * col_diff + 1.0)
    return BASE + jnp.abs(facing) * lax.rsqrt(norm)


def col_diffs(tiles, before, after, lane):
    wide = (before, *tiles, after)
    out = []
    for k in range(1, len(wide) - 1):
        nxt = pltpu.roll(jnp.where(lane == 0, wide[k + 1], wide[k]), LANES - 1, 1)
        prev = pltpu.roll(jnp.where(lane == LANES - 1, wide[k - 1], wide[k]), 1, 1)
        out.append(nxt - prev)
    return out


def kernel(
    dims,
    volume,
    place_hbm,
    index_hbm,
    extinct_hbm,
    color_hbm,
    out,
    raw,
    vol,
    shaded,
    face_in,
    face_out,
    face,
    part1,
    part2,
    packed,
    gathered,
    place,
    index,
    extinct,
    color,
    slots,
    param_sem,
    load_sem,
    halo_send,
    halo_recv,
    f1_send,
    f1_recv,
    f2_send,
    f2_recv,
    m1_send,
    m1_recv,
    m2_send,
    m2_recv,
    out_send,
    out_recv,
):
    tiles_n, slabs, rows, planes, cols = dims
    ct = cols // LANES
    blocks = rows // SUB
    me = lax.axis_index("depth")
    tile = lax.axis_index("tile")
    below = lax.rem(tile + 1, tiles_n)
    above = lax.rem(tile + tiles_n - 1, tiles_n)

    def depth_peer(j):
        return lax.rem(me + j, slabs)

    def tile_peer(j):
        return lax.rem(tile + j, tiles_n)

    params = [
        pltpu.make_async_copy(src, dst, param_sem.at[i])
        for i, (src, dst) in enumerate(
            ((place_hbm, place), (index_hbm, index), (extinct_hbm, extinct), (color_hbm, color))
        )
    ]
    def columns(c):
        return pl.ds(pl.multiple_of(c * LANES, LANES), LANES)

    def load(c):
        return pltpu.make_async_copy(
            volume.at[:, :, columns(c)],
            raw.at[c],
            load_sem.at[c],
        )

    for c in range(ct):
        load(c).start()
    for copy in params:
        copy.start()

    barrier = pltpu.get_barrier_semaphore()
    for j in range(1, slabs):
        pl.semaphore_signal(
            barrier, inc=1, device_id={"depth": depth_peer(j)}, device_id_type=MESH
        )
    for j in range(1, tiles_n):
        pl.semaphore_signal(barrier, inc=1, device_id={"tile": tile_peer(j)}, device_id_type=MESH)

    for copy in params:
        copy.wait()
    slots[0] = slabs
    slots[slabs + 1] = slabs
    for p in range(slabs):
        found = jnp.int32(0)
        for s in range(slabs):
            found = jnp.where(place[s] == p, jnp.int32(s), found)
        slots[p + 1] = found
    zero = jnp.zeros((SUB, LANES), jnp.float32)
    for side in range(2):
        for b in range(blocks):
            face_in[slabs, side, pl.ds(b * SUB, SUB), :] = zero

    pl.semaphore_wait(barrier, slabs - 1 + tiles_n - 1)

    def halo(side, c):
        row = rows - 1 if side == 0 else 0
        return pltpu.make_async_remote_copy(
            src_ref=volume.at[row, :, columns(c)],
            dst_ref=vol.at[c, pl.ds(side, planes), 0 if side else SUB - 1, :],
            send_sem=halo_send.at[side, c],
            recv_sem=halo_recv.at[side, c],
            device_id={"tile": above if side else below},
            device_id_type=MESH,
        )

    def face_first(j, side):
        owner = depth_peer(j)
        src = volume.at[
            :, side * (planes - 1), columns(owner)
        ]
        if j == 0:
            return pltpu.make_async_copy(src, face_in.at[me, side], f1_send.at[0, side])
        return pltpu.make_async_remote_copy(
            src_ref=src,
            dst_ref=face_in.at[me, side],
            send_sem=f1_send.at[j, side],
            recv_sem=f1_recv.at[j, side],
            device_id={"depth": owner},
            device_id_type=MESH,
        )

    def face_second(j):
        return pltpu.make_async_remote_copy(
            src_ref=face_out.at[j],
            dst_ref=face.at[me],
            send_sem=f2_send.at[j],
            recv_sem=f2_recv.at[j],
            device_id={"depth": depth_peer(j)},
            device_id_type=MESH,
        )

    for j in range(slabs):
        for side in range(2):
            face_first(j, side).start()

    @pl.when(tile < tiles_n - 1)
    def _():
        for c in range(ct):
            halo(0, c).start()

    @pl.when(tile > 0)
    def _():
        for c in range(ct):
            halo(1, c).start()

    pitch = rows + SUB
    flat = vol.reshape(ct, (planes + 1) * pitch, LANES)

    def view(p, c, b, shift):
        if shift == 0:
            return flat[c, pl.ds(pl.multiple_of(p * pitch + (b + 1) * SUB, SUB), SUB), :]
        window = flat.at[c, pl.ds(pl.multiple_of(p * pitch + b * SUB, SUB), 3 * SUB), :]
        return window[SUB + shift : 2 * SUB + shift, :]

    def planes_of(q, row):
        return pl.ds(q * SUB * pitch + row, SUB, stride=pitch)

    lane = lax.broadcasted_iota(jnp.int32, (SUB, LANES), 1)
    sub = lax.broadcasted_iota(jnp.int32, (SUB, LANES), 0)

    run = 2

    def shade_run(first, count, b, unroll):
        tiles = range(first, first + count)

        def step(i, carry):
            p = i + 1
            prev, here = carry[:count], carry[count:]
            nxt = tuple(view(p + 1, c, b, 0) for c in tiles)
            before = view(p, first - 1, b, 0) if first else zero
            after = view(p, first + count, b, 0) if first + count < ct else zero
            diffs = col_diffs(here, before, after, lane)
            for k, c in enumerate(tiles):
                shaded[b, c, p] = shade(
                    view(p, c, b, 1) - view(p, c, b, -1), nxt[k] - prev[k], diffs[k]
                )
            return tuple(here) + nxt

        first_two = tuple(view(p, c, b, 0) for p in range(2) for c in tiles)
        lax.fori_loop(0, planes - 2, step, first_two, unroll=unroll)

    def shade_inner(first):
        def block(b, _):
            shade_run(first, run, b, 31)
            return 0

        lax.fori_loop(1, blocks - 1, block, 0)

    pieces = planes // SUB

    def extremes_block(c, carry):
        load(c).wait()

        def step(r, carry):
            high, low = carry
            new_high, new_low = [], []
            for q in range(pieces):
                half = raw[c, r, pl.ds(q * SUB, SUB), :] * 0.5
                flat[c, planes_of(q, SUB + r), :] = half
                new_high.append(jnp.maximum(high[q], half))
                new_low.append(jnp.minimum(low[q], half))
            return tuple(new_high), tuple(new_low)

        return lax.fori_loop(0, rows, step, carry, unroll=4)

    start = (tuple([full(-BIG)] * pieces), tuple([full(BIG)] * pieces))
    extremes = lax.fori_loop(0, run + 1, extremes_block, start)
    shade_inner(0)
    extremes = lax.fori_loop(run + 1, 2 * run + 1, extremes_block, extremes)
    shade_inner(run)
    high, low = lax.fori_loop(2 * run + 1, ct, extremes_block, extremes)
    part1[0, 0:1, :] = jnp.max(functools.reduce(jnp.maximum, high), axis=0, keepdims=True)
    part1[0, 1:2, :] = -jnp.min(functools.reduce(jnp.minimum, low), axis=0, keepdims=True)

    def part_copy(stage, j):
        buf, send, recv = (part1, m1_send, m1_recv) if stage == 1 else (part2, m2_send, m2_recv)
        peer = {"depth": depth_peer(j)} if stage == 1 else {"tile": tile_peer(j)}
        return pltpu.make_async_remote_copy(
            src_ref=buf.at[0],
            dst_ref=buf.at[j],
            send_sem=send.at[j],
            recv_sem=recv.at[j],
            device_id=peer,
            device_id_type=MESH,
        )

    for j in range(1, slabs):
        part_copy(1, j).start()

    shade_inner(2 * run)

    for j in range(slabs):
        for side in range(2):
            if j == 0:
                face_first(j, side).wait()
            else:
                face_first(j, side).wait_recv()
    for j in range(slabs):
        at = place[depth_peer(j)]
        front = slots[at]
        back = slots[at + 2]
        for b in range(blocks):
            rs = pl.ds(b * SUB, SUB)
            front_value = face_in[front, 1, rs, :] * 0.5
            back_value = face_in[back, 0, rs, :] * 0.5
            if j == 0:
                face[me, 0, rs, :] = front_value
                face[me, 1, rs, :] = back_value
            else:
                face_out[j, 0, rs, :] = front_value
                face_out[j, 1, rs, :] = back_value
        if j:
            face_second(j).start()

    shade_inner(3 * run)

    for j in range(1, slabs):
        part_copy(1, j).wait_recv()
    part2[0] = jnp.max(part1[...], axis=0)
    for j in range(1, tiles_n):
        part_copy(2, j).start()

    def halo_row(side, scale):
        def step(c, _):
            if scale:
                halo(side, c).wait_recv()
            for q in range(pieces):
                at = planes_of(q, pitch if side else SUB - 1)
                flat[c, at, :] = flat[c, at, :] * 0.5 if scale else zero
            return 0

        lax.fori_loop(0, ct, step, 0)

    @pl.when(tile > 0)
    def _():
        halo_row(0, True)

    @pl.when(tile == 0)
    def _():
        halo_row(0, False)

    @pl.when(tile < tiles_n - 1)
    def _():
        halo_row(1, True)

    @pl.when(tile == tiles_n - 1)
    def _():
        halo_row(1, False)

    def outer(i, _):
        shade_run(0, ct, i * (blocks - 1), 31)
        return 0

    lax.fori_loop(0, 2, outer, 0)

    for j in range(1, slabs):
        face_second(j).wait_recv()

    def edge_planes(b, _):
        rs = pl.ds(pl.multiple_of(b * SUB, SUB), SUB)
        for side in range(2):
            p = side * (planes - 1)
            diffs = col_diffs([view(p, c, b, 0) for c in range(ct)], zero, zero, lane)
            for c in range(ct):
                other = face[c, side, rs, :]
                if side == 0:
                    plane_diff = view(1, c, b, 0) - other
                else:
                    plane_diff = other - view(planes - 2, c, b, 0)
                shaded[b, c, p] = shade(view(p, c, b, 1) - view(p, c, b, -1), plane_diff, diffs[c])
        return 0

    lax.fori_loop(0, blocks, edge_planes, 0)

    def by_segment(values):
        table = full(values[0])
        for s in range(1, len(values)):
            table = jnp.where(sub == s, values[s], table)
        return table

    knots = index.shape[0]
    points = [index[k].astype(jnp.float32) for k in range(knots)]
    lower = by_segment(points[:-1])
    upper = by_segment(points[1:])
    width = jnp.where(sub < knots - 1, upper - lower, 1.0)
    offsets, slopes = [], []
    for channel in range(4):
        scale = -LOG2E if channel == 0 else KC
        values = [
            extinct[k] if channel == 0 else color[channel - 1, k] for k in range(knots)
        ]
        begin, end = by_segment(values[:-1]), by_segment(values[1:])
        slope = (end - begin) / width
        offsets.append((begin - slope * lower) * scale)
        slopes.append(slope * scale)

    for j in range(1, tiles_n):
        part_copy(2, j).wait_recv()
    extremes = jnp.max(jnp.max(part2[...], axis=0), axis=1, keepdims=True)
    extremes = jnp.broadcast_to(extremes, (2, LANES))
    low_value = jnp.broadcast_to(-extremes[1:2, :], (SUB, LANES))
    span = jnp.broadcast_to(extremes[0:1, :] + extremes[1:2, :], (SUB, LANES)) + 0.5
    unit = span * (1.0 / (TABLE - 1.0))
    slopes = [slope * ((TABLE - 1.0) / span) for slope in slopes]
    bounds = [points[k] * unit for k in range(1, knots - 1)]
    odd = jnp.where(sub >= 6, BIG, jnp.where(sub >= 4, bounds[4], jnp.where(sub >= 2, bounds[2], bounds[0])))

    cores = 2
    chips = slabs // cores
    chip = me // cores
    mate = me + 1 - 2 * lax.rem(me, cores)
    pair = 2

    def render(owner, result):
        def rows_pair(i, _):
            def step(p, carry):
                out_carry = []
                for k in range(pair):
                    b = i * pair + k
                    through, sums = carry[k]
                    dist = view(p, owner, b, 0) - low_value
                    even = jnp.where(dist >= bounds[1], 2, 0)
                    even = jnp.where(dist >= bounds[3], 4, even)
                    even = jnp.where(dist >= bounds[5], 6, even)
                    segment = jnp.where(dist >= lookup(odd, even), even + 1, even)
                    offset = [lookup(t, segment) for t in offsets]
                    slope = [lookup(t, segment) for t in slopes]
                    rest = through * jnp.exp2(offset[0] + slope[0] * dist)
                    weight = (through - rest) * shaded[b, owner, p]
                    sums = tuple(
                        sums[n] + weight * (offset[n + 1] + slope[n + 1] * dist)
                        for n in range(3)
                    )
                    out_carry.append((rest, sums))
                return tuple(out_carry)

            begin = tuple((full(1.0), (full(0.0),) * 3) for _ in range(pair))
            done = lax.fori_loop(0, planes, step, begin, unroll=32)
            for k in range(pair):
                for n in range(3):
                    result[owner, i * pair + k, n] = done[k][1][n]
                result[owner, i * pair + k, 3] = done[k][0]
            return 0

        lax.fori_loop(0, blocks // pair, rows_pair, 0)

    def result_copy(owner, sender):
        return pltpu.make_async_remote_copy(
            src_ref=packed.at[owner],
            dst_ref=gathered.at[sender],
            send_sem=out_send.at[owner],
            recv_sem=out_recv.at[sender],
            device_id={"depth": owner},
            device_id_type=MESH,
        )

    def away(i, _):
        n = i // cores
        owner = cores * lax.rem(chip + 2 + (3 * n * n - 5 * n) // 2, chips) + i % cores
        render(owner, packed)
        result_copy(owner, me).start()
        return 0

    lax.fori_loop(0, slabs - cores, away, 0)
    render(mate, packed)
    result_copy(mate, me).start()
    render(me, gathered)

    @pl.when(tile < tiles_n - 1)
    def _():
        for c in range(ct):
            halo(0, c).wait_send()

    @pl.when(tile > 0)
    def _():
        for c in range(ct):
            halo(1, c).wait_send()

    for j in range(1, slabs):
        for side in range(2):
            face_first(j, side).wait_send()
        face_second(j).wait_send()
        part_copy(1, j).wait_send()
    for j in range(1, tiles_n):
        part_copy(2, j).wait_send()

    for j in range(1, slabs):
        result_copy(depth_peer(j), me).wait_send()
    for j in range(1, slabs):
        result_copy(depth_peer(j), depth_peer(j)).wait_recv()

    def composite(b, _):
        rs = pl.ds(pl.multiple_of(b * SUB, SUB), SUB)
        through = full(1.0)
        sums = [full(0.0)] * 3
        for p in range(slabs):
            slot = slots[p + 1]
            for i in range(3):
                sums[i] = sums[i] + through * gathered[slot, b, i]
            through = through * gathered[slot, b, 3]
        for i in range(3):
            out[i, rs, :] = sums[i]
        return 0

    lax.fori_loop(0, blocks, composite, 0)


def solution(mesh):
    tiles_n, slabs = mesh.shape["tile"], mesh.shape["depth"]

    def body(volume, slab_place, control_index, control_extinction, control_color):
        rows, planes, cols = volume.shape
        ct, blocks = cols // LANES, rows // SUB
        dims = (tiles_n, slabs, rows, planes, cols)
        f32, dma = jnp.float32, pltpu.SemaphoreType.DMA
        return pl.pallas_call(
            functools.partial(kernel, dims),
            out_shape=jax.ShapeDtypeStruct((3, rows, cols // slabs), f32),
            in_specs=[pl.BlockSpec(memory_space=pltpu.HBM)] * 5,
            out_specs=pl.BlockSpec(memory_space=pltpu.VMEM),
            scratch_shapes=[
                pltpu.VMEM((ct, rows, planes, LANES), f32),
                pltpu.VMEM((ct, planes + 1, rows + SUB, LANES), f32),
                pltpu.VMEM((blocks, ct, planes, SUB, LANES), f32),
                pltpu.VMEM((slabs + 1, 2, rows, LANES), f32),
                pltpu.VMEM((slabs, 2, rows, LANES), f32),
                pltpu.VMEM((slabs, 2, rows, LANES), f32),
                pltpu.VMEM((slabs, 2, LANES), f32),
                pltpu.VMEM((tiles_n, 2, LANES), f32),
                pltpu.VMEM((slabs, blocks, 4, SUB, LANES), f32),
                pltpu.VMEM((slabs, blocks, 4, SUB, LANES), f32),
                pltpu.SMEM(slab_place.shape, jnp.int32),
                pltpu.SMEM(control_index.shape, jnp.int32),
                pltpu.SMEM(control_extinction.shape, f32),
                pltpu.SMEM(control_color.shape, f32),
                pltpu.SMEM((slabs + 2,), jnp.int32),
                dma((4,)),
                dma((ct,)),
                dma((2, ct)),
                dma((2, ct)),
                dma((slabs, 2)),
                dma((slabs, 2)),
                dma((slabs,)),
                dma((slabs,)),
                dma((slabs,)),
                dma((slabs,)),
                dma((tiles_n,)),
                dma((tiles_n,)),
                dma((slabs,)),
                dma((slabs,)),
            ],
            compiler_params=pltpu.CompilerParams(
                collective_id=0, has_side_effects=True, vmem_limit_bytes=48 << 20
            ),
            name="render",
        )(
            volume,
            *(
                pltpu.with_memory_space_constraint(x, pltpu.HBM)
                for x in (slab_place, control_index, control_extinction, control_color)
            ),
        )

    placed = (P("tile", "depth", None), P(), P(), P(), P())
    return jax.shard_map(
        body, mesh=mesh, in_specs=placed, out_specs=P(None, "tile", "depth"), check_vma=False
    )
```

```python
import functools

import jax
import jax.numpy as jnp
import numpy as np
from jax import lax
from jax.experimental import pallas as pl
from jax.experimental.pallas import tpu as pltpu
from jax.sharding import PartitionSpec as P

MESH = pl.DeviceIdType.MESH
TABLE = 256
LANES = 128
SUB = 8
KA, KB, KC = 0.48 / 0.64, 0.6 / 0.64, 0.7 * 0.64
BASE = 0.3 / KC
LOG2E = float(np.log2(np.e))
BIG = 3.0e38


def full(value):
    return jnp.full((SUB, LANES), value, jnp.float32)


def lookup(table, index):
    dims = lax.GatherDimensionNumbers(
        offset_dims=(),
        collapsed_slice_dims=(0,),
        start_index_map=(0,),
        operand_batching_dims=(1,),
        start_indices_batching_dims=(1,),
    )
    return lax.gather(
        table, index[..., None], dims, (1, 1), mode=lax.GatherScatterMode.PROMISE_IN_BOUNDS
    )


def shade(row_diff, plane_diff, col_diff):
    facing = (col_diff + KB * plane_diff) + KA * row_diff
    norm = (row_diff * row_diff + plane_diff * plane_diff) + (col_diff * col_diff + 1.0)
    return BASE + jnp.abs(facing) * lax.rsqrt(norm)


def col_diffs(tiles, before, after, lane):
    wide = (before, *tiles, after)
    out = []
    for k in range(1, len(wide) - 1):
        nxt = pltpu.roll(jnp.where(lane == 0, wide[k + 1], wide[k]), LANES - 1, 1)
        prev = pltpu.roll(jnp.where(lane == LANES - 1, wide[k - 1], wide[k]), 1, 1)
        out.append(nxt - prev)
    return out


def kernel(
    dims,
    volume,
    place_hbm,
    index_hbm,
    extinct_hbm,
    color_hbm,
    out,
    raw,
    vol,
    shaded,
    face_in,
    face_out,
    face,
    part1,
    part2,
    packed,
    gathered,
    place,
    index,
    extinct,
    color,
    slots,
    param_sem,
    load_sem,
    halo_send,
    halo_recv,
    f1_own,
    f1_send,
    f1_recv,
    f2_send,
    f2_recv,
    m1_send,
    m1_recv,
    m2_send,
    m2_recv,
    out_send,
    out_recv,
):
    tiles_n, slabs, rows, planes, cols = dims
    ct = cols // LANES
    blocks = rows // SUB
    me = lax.axis_index("depth")
    tile = lax.axis_index("tile")
    below = lax.rem(tile + 1, tiles_n)
    above = lax.rem(tile + tiles_n - 1, tiles_n)

    def depth_peer(j):
        return lax.rem(me + j, slabs)

    def tile_peer(j):
        return lax.rem(tile + j, tiles_n)

    def wait_all(like, sem):
        pltpu.make_async_copy(like, like, sem).wait()

    params = [
        pltpu.make_async_copy(src, dst, param_sem.at[i])
        for i, (src, dst) in enumerate(
            ((place_hbm, place), (index_hbm, index), (extinct_hbm, extinct), (color_hbm, color))
        )
    ]
    def columns(c):
        return pl.ds(pl.multiple_of(c * LANES, LANES), LANES)

    def load(c):
        return pltpu.make_async_copy(
            volume.at[:, :, columns(c)],
            raw.at[c],
            load_sem.at[c],
        )

    for c in range(ct):
        load(c).start()
    for copy in params:
        copy.start()

    barrier = pltpu.get_barrier_semaphore()
    for j in range(1, slabs):
        pl.semaphore_signal(
            barrier, inc=1, device_id={"depth": depth_peer(j)}, device_id_type=MESH
        )
    for j in range(1, tiles_n):
        pl.semaphore_signal(barrier, inc=1, device_id={"tile": tile_peer(j)}, device_id_type=MESH)

    for copy in params:
        copy.wait()
    slots[0] = slabs
    slots[slabs + 1] = slabs
    for p in range(slabs):
        found = jnp.int32(0)
        for s in range(slabs):
            found = jnp.where(place[s] == p, jnp.int32(s), found)
        slots[p + 1] = found
    zero = jnp.zeros((SUB, LANES), jnp.float32)
    for side in range(2):
        for b in range(blocks):
            face_in[slabs, side, pl.ds(b * SUB, SUB), :] = zero

    pl.semaphore_wait(barrier, slabs - 1 + tiles_n - 1)

    def halo(side, c):
        row = rows - 1 if side == 0 else 0
        return pltpu.make_async_remote_copy(
            src_ref=volume.at[row, :, columns(c)],
            dst_ref=vol.at[c, pl.ds(side, planes), 0 if side else SUB - 1, :],
            send_sem=halo_send.at[side],
            recv_sem=halo_recv.at[side],
            device_id={"tile": above if side else below},
            device_id_type=MESH,
        )

    def face_first(j, side):
        owner = depth_peer(j)
        src = volume.at[
            :, side * (planes - 1), columns(owner)
        ]
        if j == 0:
            return pltpu.make_async_copy(src, face_in.at[me, side], f1_own)
        return pltpu.make_async_remote_copy(
            src_ref=src,
            dst_ref=face_in.at[me, side],
            send_sem=f1_send,
            recv_sem=f1_recv,
            device_id={"depth": owner},
            device_id_type=MESH,
        )

    def face_second(j):
        return pltpu.make_async_remote_copy(
            src_ref=face_out.at[j],
            dst_ref=face.at[me],
            send_sem=f2_send,
            recv_sem=f2_recv,
            device_id={"depth": depth_peer(j)},
            device_id_type=MESH,
        )

    for j in range(slabs):
        for side in range(2):
            face_first(j, side).start()

    @pl.when(tile < tiles_n - 1)
    def _():
        for c in range(ct):
            halo(0, c).start()

    @pl.when(tile > 0)
    def _():
        for c in range(ct):
            halo(1, c).start()

    pitch = rows + SUB
    flat = vol.reshape(ct, (planes + 1) * pitch, LANES)

    def view(p, c, b, shift):
        if shift == 0:
            return flat[c, pl.ds(pl.multiple_of(p * pitch + (b + 1) * SUB, SUB), SUB), :]
        window = flat.at[c, pl.ds(pl.multiple_of(p * pitch + b * SUB, SUB), 3 * SUB), :]
        return window[SUB + shift : 2 * SUB + shift, :]

    def planes_of(q, row):
        return pl.ds(q * SUB * pitch + row, SUB, stride=pitch)

    lane = lax.broadcasted_iota(jnp.int32, (SUB, LANES), 1)
    sub = lax.broadcasted_iota(jnp.int32, (SUB, LANES), 0)

    run = 2

    def shade_run(first, count, b, unroll):
        tiles = range(first, first + count)

        def step(i, carry):
            p = i + 1
            prev, here = carry[:count], carry[count:]
            nxt = tuple(view(p + 1, c, b, 0) for c in tiles)
            before = view(p, first - 1, b, 0) if first else zero
            after = view(p, first + count, b, 0) if first + count < ct else zero
            diffs = col_diffs(here, before, after, lane)
            for k, c in enumerate(tiles):
                shaded[b, c, p] = shade(
                    view(p, c, b, 1) - view(p, c, b, -1), nxt[k] - prev[k], diffs[k]
                )
            return tuple(here) + nxt

        first_two = tuple(view(p, c, b, 0) for p in range(2) for c in tiles)
        lax.fori_loop(0, planes - 2, step, first_two, unroll=unroll)

    def shade_inner(first):
        def block(b, _):
            shade_run(first, run, b, planes - 2)
            return 0

        lax.fori_loop(1, blocks - 1, block, 0)

    pieces = planes // SUB

    def extremes_block(c, carry):
        load(c).wait()

        def step(r, carry):
            high, low = carry
            new_high, new_low = [], []
            for q in range(pieces):
                half = raw[c, r, pl.ds(q * SUB, SUB), :] * 0.5
                flat[c, planes_of(q, SUB + r), :] = half
                new_high.append(jnp.maximum(high[q], half))
                new_low.append(jnp.minimum(low[q], half))
            return tuple(new_high), tuple(new_low)

        return lax.fori_loop(0, rows, step, carry, unroll=4)

    start = (tuple([full(-BIG)] * pieces), tuple([full(BIG)] * pieces))
    extremes = lax.fori_loop(0, run + 1, extremes_block, start)
    shade_inner(0)
    extremes = lax.fori_loop(run + 1, 2 * run + 1, extremes_block, extremes)
    shade_inner(run)
    high, low = lax.fori_loop(2 * run + 1, ct, extremes_block, extremes)
    part1[0, 0:1, :] = jnp.max(functools.reduce(jnp.maximum, high), axis=0, keepdims=True)
    part1[0, 1:2, :] = -jnp.min(functools.reduce(jnp.minimum, low), axis=0, keepdims=True)

    def part_copy(stage, j):
        buf, send, recv = (part1, m1_send, m1_recv) if stage == 1 else (part2, m2_send, m2_recv)
        peer = {"depth": depth_peer(j)} if stage == 1 else {"tile": tile_peer(j)}
        return pltpu.make_async_remote_copy(
            src_ref=buf.at[0],
            dst_ref=buf.at[j],
            send_sem=send,
            recv_sem=recv,
            device_id=peer,
            device_id_type=MESH,
        )

    for j in range(1, slabs):
        part_copy(1, j).start()

    shade_inner(2 * run)

    others = slabs - 1
    wait_all(face_in.at[0], f1_own)
    wait_all(face_in.at[pl.ds(0, others)], f1_recv)
    for j in range(slabs):
        at = place[depth_peer(j)]
        front = slots[at]
        back = slots[at + 2]
        for b in range(blocks):
            rs = pl.ds(b * SUB, SUB)
            front_value = face_in[front, 1, rs, :] * 0.5
            back_value = face_in[back, 0, rs, :] * 0.5
            if j == 0:
                face[me, 0, rs, :] = front_value
                face[me, 1, rs, :] = back_value
            else:
                face_out[j, 0, rs, :] = front_value
                face_out[j, 1, rs, :] = back_value
        if j:
            face_second(j).start()

    shade_inner(3 * run)

    wait_all(part1.at[pl.ds(1, others)], m1_recv)
    part2[0] = jnp.max(part1[...], axis=0)
    for j in range(1, tiles_n):
        part_copy(2, j).start()

    def halo_row(side, scale):
        if scale:
            wait_all(vol.at[:, pl.ds(side, planes), 0 if side else SUB - 1, :], halo_recv.at[side])

        def step(c, _):
            for q in range(pieces):
                at = planes_of(q, pitch if side else SUB - 1)
                flat[c, at, :] = flat[c, at, :] * 0.5 if scale else zero
            return 0

        lax.fori_loop(0, ct, step, 0)

    @pl.when(tile > 0)
    def _():
        halo_row(0, True)

    @pl.when(tile == 0)
    def _():
        halo_row(0, False)

    @pl.when(tile < tiles_n - 1)
    def _():
        halo_row(1, True)

    @pl.when(tile == tiles_n - 1)
    def _():
        halo_row(1, False)

    def outer(i, _):
        shade_run(0, ct, i * (blocks - 1), 31)
        return 0

    lax.fori_loop(0, 2, outer, 0)

    wait_all(face.at[pl.ds(0, others)], f2_recv)

    def edge_planes(b, _):
        rs = pl.ds(pl.multiple_of(b * SUB, SUB), SUB)
        for side in range(2):
            p = side * (planes - 1)
            diffs = col_diffs([view(p, c, b, 0) for c in range(ct)], zero, zero, lane)
            for c in range(ct):
                other = face[c, side, rs, :]
                if side == 0:
                    plane_diff = view(1, c, b, 0) - other
                else:
                    plane_diff = other - view(planes - 2, c, b, 0)
                shaded[b, c, p] = shade(view(p, c, b, 1) - view(p, c, b, -1), plane_diff, diffs[c])
        return 0

    lax.fori_loop(0, blocks, edge_planes, 0)

    def by_segment(values):
        table = full(values[0])
        for s in range(1, len(values)):
            table = jnp.where(sub == s, values[s], table)
        return table

    knots = index.shape[0]
    points = [index[k].astype(jnp.float32) for k in range(knots)]
    lower = by_segment(points[:-1])
    upper = by_segment(points[1:])
    width = jnp.where(sub < knots - 1, upper - lower, 1.0)
    offsets, slopes = [], []
    for channel in range(4):
        scale = -LOG2E if channel == 0 else KC
        values = [
            extinct[k] if channel == 0 else color[channel - 1, k] for k in range(knots)
        ]
        begin, end = by_segment(values[:-1]), by_segment(values[1:])
        slope = (end - begin) / width
        offsets.append((begin - slope * lower) * scale)
        slopes.append(slope * scale)

    wait_all(part2.at[pl.ds(1, tiles_n - 1)], m2_recv)
    extremes = jnp.max(jnp.max(part2[...], axis=0), axis=1, keepdims=True)
    extremes = jnp.broadcast_to(extremes, (2, LANES))
    low_value = jnp.broadcast_to(-extremes[1:2, :], (SUB, LANES))
    span = jnp.broadcast_to(extremes[0:1, :] + extremes[1:2, :], (SUB, LANES)) + 0.5
    unit = span * (1.0 / (TABLE - 1.0))
    slopes = [slope * ((TABLE - 1.0) / span) for slope in slopes]
    bounds = [points[k] * unit for k in range(1, knots - 1)]
    odd = jnp.where(sub >= 6, BIG, jnp.where(sub >= 4, bounds[4], jnp.where(sub >= 2, bounds[2], bounds[0])))

    cores = 2
    chips = slabs // cores
    chip = me // cores
    mate = me + 1 - 2 * lax.rem(me, cores)
    pair = 2

    def render(owner, result):
        def rows_pair(i, _):
            def step(p, carry):
                out_carry = []
                for k in range(pair):
                    b = i * pair + k
                    through, sums = carry[k]
                    dist = view(p, owner, b, 0) - low_value
                    even = jnp.where(dist >= bounds[1], 2, 0)
                    even = jnp.where(dist >= bounds[3], 4, even)
                    even = jnp.where(dist >= bounds[5], 6, even)
                    segment = jnp.where(dist >= lookup(odd, even), even + 1, even)
                    offset = [lookup(t, segment) for t in offsets]
                    slope = [lookup(t, segment) for t in slopes]
                    rest = through * jnp.exp2(offset[0] + slope[0] * dist)
                    weight = (through - rest) * shaded[b, owner, p]
                    sums = tuple(
                        sums[n] + weight * (offset[n + 1] + slope[n + 1] * dist)
                        for n in range(3)
                    )
                    out_carry.append((rest, sums))
                return tuple(out_carry)

            begin = tuple((full(1.0), (full(0.0),) * 3) for _ in range(pair))
            done = lax.fori_loop(0, planes, step, begin, unroll=32)
            for k in range(pair):
                for n in range(3):
                    result[owner, i * pair + k, n] = done[k][1][n]
                result[owner, i * pair + k, 3] = done[k][0]
            return 0

        lax.fori_loop(0, blocks // pair, rows_pair, 0)

    def result_copy(owner):
        return pltpu.make_async_remote_copy(
            src_ref=packed.at[owner],
            dst_ref=gathered.at[me],
            send_sem=out_send,
            recv_sem=out_recv,
            device_id={"depth": owner},
            device_id_type=MESH,
        )

    def away(i, _):
        n = i // cores
        owner = cores * lax.rem(chip + 2 + (3 * n * n - 5 * n) // 2, chips) + i % cores
        render(owner, packed)
        result_copy(owner).start()
        return 0

    lax.fori_loop(0, slabs - cores, away, 0)
    render(mate, packed)
    result_copy(mate).start()
    render(me, gathered)

    @pl.when(tile < tiles_n - 1)
    def _():
        wait_all(volume.at[rows - 1], halo_send.at[0])

    @pl.when(tile > 0)
    def _():
        wait_all(volume.at[0], halo_send.at[1])

    wait_all(face_in.at[pl.ds(0, others)], f1_send)
    wait_all(face_out.at[pl.ds(0, others)], f2_send)
    wait_all(part1.at[pl.ds(1, others)], m1_send)
    wait_all(part2.at[pl.ds(1, tiles_n - 1)], m2_send)
    wait_all(packed.at[pl.ds(0, others)], out_send)

    wait_all(gathered.at[pl.ds(0, others)], out_recv)

    def composite(b, _):
        rs = pl.ds(pl.multiple_of(b * SUB, SUB), SUB)
        through = full(1.0)
        sums = [full(0.0)] * 3
        for p in range(slabs):
            slot = slots[p + 1]
            for i in range(3):
                sums[i] = sums[i] + through * gathered[slot, b, i]
            through = through * gathered[slot, b, 3]
        for i in range(3):
            out[i, rs, :] = sums[i]
        return 0

    lax.fori_loop(0, blocks, composite, 0)


def solution(mesh):
    tiles_n, slabs = mesh.shape["tile"], mesh.shape["depth"]

    def body(volume, slab_place, control_index, control_extinction, control_color):
        rows, planes, cols = volume.shape
        ct, blocks = cols // LANES, rows // SUB
        dims = (tiles_n, slabs, rows, planes, cols)
        f32, dma = jnp.float32, pltpu.SemaphoreType.DMA
        return pl.pallas_call(
            functools.partial(kernel, dims),
            out_shape=jax.ShapeDtypeStruct((3, rows, cols // slabs), f32),
            in_specs=[pl.BlockSpec(memory_space=pltpu.HBM)] * 5,
            out_specs=pl.BlockSpec(memory_space=pltpu.VMEM),
            scratch_shapes=[
                pltpu.VMEM((ct, rows, planes, LANES), f32),
                pltpu.VMEM((ct, planes + 1, rows + SUB, LANES), f32),
                pltpu.VMEM((blocks, ct, planes, SUB, LANES), f32),
                pltpu.VMEM((slabs + 1, 2, rows, LANES), f32),
                pltpu.VMEM((slabs, 2, rows, LANES), f32),
                pltpu.VMEM((slabs, 2, rows, LANES), f32),
                pltpu.VMEM((slabs, 2, LANES), f32),
                pltpu.VMEM((tiles_n, 2, LANES), f32),
                pltpu.VMEM((slabs, blocks, 4, SUB, LANES), f32),
                pltpu.VMEM((slabs, blocks, 4, SUB, LANES), f32),
                pltpu.SMEM(slab_place.shape, jnp.int32),
                pltpu.SMEM(control_index.shape, jnp.int32),
                pltpu.SMEM(control_extinction.shape, f32),
                pltpu.SMEM(control_color.shape, f32),
                pltpu.SMEM((slabs + 2,), jnp.int32),
                dma((4,)),
                dma((ct,)),
                dma((2,)),
                dma((2,)),
                *[dma(())] * 11,
            ],
            compiler_params=pltpu.CompilerParams(
                collective_id=0, has_side_effects=True, vmem_limit_bytes=48 << 20
            ),
            name="render",
        )(
            volume,
            *(
                pltpu.with_memory_space_constraint(x, pltpu.HBM)
                for x in (slab_place, control_index, control_extinction, control_color)
            ),
        )

    placed = (P("tile", "depth", None), P(), P(), P(), P())
    return jax.shard_map(
        body, mesh=mesh, in_specs=placed, out_specs=P(None, "tile", "depth"), check_vma=False
    )
```

```python
import functools

import jax
import jax.numpy as jnp
import numpy as np
from jax import lax
from jax.experimental import pallas as pl
from jax.experimental.pallas import tpu as pltpu
from jax.sharding import PartitionSpec as P

MESH = pl.DeviceIdType.MESH
TABLE = 256
LANES = 128
SUB = 8
KA, KB, KC = 0.48 / 0.64, 0.6 / 0.64, 0.7 * 0.64
BASE = 0.3 / KC
LOG2E = float(np.log2(np.e))
BIG = 3.0e38


def full(value):
    return jnp.full((SUB, LANES), value, jnp.float32)


def lookup(table, index):
    dims = lax.GatherDimensionNumbers(
        offset_dims=(),
        collapsed_slice_dims=(0,),
        start_index_map=(0,),
        operand_batching_dims=(1,),
        start_indices_batching_dims=(1,),
    )
    return lax.gather(
        table, index[..., None], dims, (1, 1), mode=lax.GatherScatterMode.PROMISE_IN_BOUNDS
    )


def shade(row_diff, plane_diff, col_diff):
    facing = (col_diff + KB * plane_diff) + KA * row_diff
    norm = (row_diff * row_diff + plane_diff * plane_diff) + (col_diff * col_diff + 1.0)
    return BASE + jnp.abs(facing) * lax.rsqrt(norm)


def col_diffs(tiles, before, after, lane):
    wide = (before, *tiles, after)
    out = []
    for k in range(1, len(wide) - 1):
        nxt = pltpu.roll(jnp.where(lane == 0, wide[k + 1], wide[k]), LANES - 1, 1)
        prev = pltpu.roll(jnp.where(lane == LANES - 1, wide[k - 1], wide[k]), 1, 1)
        out.append(nxt - prev)
    return out


def kernel(
    dims,
    volume,
    place_hbm,
    index_hbm,
    extinct_hbm,
    color_hbm,
    out,
    raw,
    vol,
    shaded,
    face_in,
    face_out,
    face,
    part1,
    part2,
    packed,
    gathered,
    place,
    index,
    extinct,
    color,
    slots,
    param_sem,
    load_sem,
    halo_send,
    halo_recv,
    f1_own,
    f1_send,
    f1_recv,
    f2_send,
    f2_recv,
    m1_send,
    m1_recv,
    m2_send,
    m2_recv,
    out_send,
    out_recv,
):
    tiles_n, slabs, rows, planes, cols = dims
    ct = cols // LANES
    blocks = rows // SUB
    me = lax.axis_index("depth")
    tile = lax.axis_index("tile")
    below = lax.rem(tile + 1, tiles_n)
    above = lax.rem(tile + tiles_n - 1, tiles_n)

    def depth_peer(j):
        return lax.rem(me + j, slabs)

    def tile_peer(j):
        return lax.rem(tile + j, tiles_n)

    def wait_all(like, sem):
        pltpu.make_async_copy(like, like, sem).wait()

    params = [
        pltpu.make_async_copy(src, dst, param_sem.at[i])
        for i, (src, dst) in enumerate(
            ((place_hbm, place), (index_hbm, index), (extinct_hbm, extinct), (color_hbm, color))
        )
    ]
    def columns(c):
        return pl.ds(pl.multiple_of(c * LANES, LANES), LANES)

    def load(c):
        return pltpu.make_async_copy(
            volume.at[:, :, columns(c)],
            raw.at[c],
            load_sem.at[c],
        )

    for c in range(ct):
        load(c).start()
    for copy in params:
        copy.start()

    barrier = pltpu.get_barrier_semaphore()
    for j in range(1, slabs):
        pl.semaphore_signal(
            barrier, inc=1, device_id={"depth": depth_peer(j)}, device_id_type=MESH
        )
    for j in range(1, tiles_n):
        pl.semaphore_signal(barrier, inc=1, device_id={"tile": tile_peer(j)}, device_id_type=MESH)

    for copy in params:
        copy.wait()
    slots[0] = slabs
    slots[slabs + 1] = slabs
    for p in range(slabs):
        found = jnp.int32(0)
        for s in range(slabs):
            found = jnp.where(place[s] == p, jnp.int32(s), found)
        slots[p + 1] = found
    zero = jnp.zeros((SUB, LANES), jnp.float32)
    for side in range(2):
        for b in range(blocks):
            face_in[slabs, side, pl.ds(b * SUB, SUB), :] = zero

    pl.semaphore_wait(barrier, slabs - 1 + tiles_n - 1)

    def halo(side, c):
        row = rows - 1 if side == 0 else 0
        return pltpu.make_async_remote_copy(
            src_ref=volume.at[row, :, columns(c)],
            dst_ref=vol.at[c, pl.ds(side, planes), 0 if side else SUB - 1, :],
            send_sem=halo_send.at[side],
            recv_sem=halo_recv.at[side],
            device_id={"tile": above if side else below},
            device_id_type=MESH,
        )

    def face_first(j, side):
        owner = depth_peer(j)
        src = volume.at[
            :, side * (planes - 1), columns(owner)
        ]
        if j == 0:
            return pltpu.make_async_copy(src, face_in.at[me, side], f1_own)
        return pltpu.make_async_remote_copy(
            src_ref=src,
            dst_ref=face_in.at[me, side],
            send_sem=f1_send,
            recv_sem=f1_recv,
            device_id={"depth": owner},
            device_id_type=MESH,
        )

    def face_second(j):
        return pltpu.make_async_remote_copy(
            src_ref=face_out.at[j],
            dst_ref=face.at[me],
            send_sem=f2_send,
            recv_sem=f2_recv,
            device_id={"depth": depth_peer(j)},
            device_id_type=MESH,
        )

    for j in range(slabs):
        for side in range(2):
            face_first(j, side).start()

    @pl.when(tile < tiles_n - 1)
    def _():
        for c in range(ct):
            halo(0, c).start()

    @pl.when(tile > 0)
    def _():
        for c in range(ct):
            halo(1, c).start()

    pitch = rows + SUB
    flat = vol.reshape(ct, (planes + 1) * pitch, LANES)

    def view(p, c, b, shift):
        if shift == 0:
            return flat[c, pl.ds(pl.multiple_of(p * pitch + (b + 1) * SUB, SUB), SUB), :]
        window = flat.at[c, pl.ds(pl.multiple_of(p * pitch + b * SUB, SUB), 3 * SUB), :]
        return window[SUB + shift : 2 * SUB + shift, :]

    def planes_of(q, row):
        return pl.ds(q * SUB * pitch + row, SUB, stride=pitch)

    lane = lax.broadcasted_iota(jnp.int32, (SUB, LANES), 1)
    sub = lax.broadcasted_iota(jnp.int32, (SUB, LANES), 0)

    run = 2

    def shade_run(first, count, b, unroll):
        tiles = range(first, first + count)

        def step(i, carry):
            p = i + 1
            prev, here = carry[:count], carry[count:]
            nxt = tuple(view(p + 1, c, b, 0) for c in tiles)
            before = view(p, first - 1, b, 0) if first else zero
            after = view(p, first + count, b, 0) if first + count < ct else zero
            diffs = col_diffs(here, before, after, lane)
            for k, c in enumerate(tiles):
                shaded[b, c, p] = shade(
                    view(p, c, b, 1) - view(p, c, b, -1), nxt[k] - prev[k], diffs[k]
                )
            return tuple(here) + nxt

        first_two = tuple(view(p, c, b, 0) for p in range(2) for c in tiles)
        lax.fori_loop(0, planes - 2, step, first_two, unroll=unroll)

    def shade_inner(first):
        def block(b, _):
            shade_run(first, run, b, planes - 2)
            return 0

        lax.fori_loop(1, blocks - 1, block, 0)

    pieces = planes // SUB

    def extremes_block(c, carry):
        load(c).wait()

        def step(r, carry):
            high, low = carry
            new_high, new_low = [], []
            for q in range(pieces):
                half = raw[c, r, pl.ds(q * SUB, SUB), :] * 0.5
                flat[c, planes_of(q, SUB + r), :] = half
                new_high.append(jnp.maximum(high[q], half))
                new_low.append(jnp.minimum(low[q], half))
            return tuple(new_high), tuple(new_low)

        return lax.fori_loop(0, rows, step, carry, unroll=4)

    start = (tuple([full(-BIG)] * pieces), tuple([full(BIG)] * pieces))
    extremes = lax.fori_loop(0, run + 1, extremes_block, start)
    shade_inner(0)
    extremes = lax.fori_loop(run + 1, 2 * run + 1, extremes_block, extremes)
    high, low = lax.fori_loop(2 * run + 1, ct, extremes_block, extremes)
    part1[0, 0:1, :] = jnp.max(functools.reduce(jnp.maximum, high), axis=0, keepdims=True)
    part1[0, 1:2, :] = -jnp.min(functools.reduce(jnp.minimum, low), axis=0, keepdims=True)

    def part_copy(stage, j):
        buf, send, recv = (part1, m1_send, m1_recv) if stage == 1 else (part2, m2_send, m2_recv)
        peer = {"depth": depth_peer(j)} if stage == 1 else {"tile": tile_peer(j)}
        return pltpu.make_async_remote_copy(
            src_ref=buf.at[0],
            dst_ref=buf.at[j],
            send_sem=send,
            recv_sem=recv,
            device_id=peer,
            device_id_type=MESH,
        )

    for j in range(1, slabs):
        part_copy(1, j).start()

    shade_inner(run)
    shade_inner(2 * run)

    others = slabs - 1
    wait_all(face_in.at[0], f1_own)
    wait_all(face_in.at[pl.ds(0, others)], f1_recv)
    for j in range(slabs):
        at = place[depth_peer(j)]
        front = slots[at]
        back = slots[at + 2]
        for b in range(blocks):
            rs = pl.ds(b * SUB, SUB)
            front_value = face_in[front, 1, rs, :] * 0.5
            back_value = face_in[back, 0, rs, :] * 0.5
            if j == 0:
                face[me, 0, rs, :] = front_value
                face[me, 1, rs, :] = back_value
            else:
                face_out[j, 0, rs, :] = front_value
                face_out[j, 1, rs, :] = back_value
        if j:
            face_second(j).start()

    shade_inner(3 * run)

    wait_all(part1.at[pl.ds(1, others)], m1_recv)
    part2[0] = jnp.max(part1[...], axis=0)
    for j in range(1, tiles_n):
        part_copy(2, j).start()

    def halo_row(side, scale):
        if scale:
            wait_all(vol.at[:, pl.ds(side, planes), 0 if side else SUB - 1, :], halo_recv.at[side])

        def step(c, _):
            for q in range(pieces):
                at = planes_of(q, pitch if side else SUB - 1)
                flat[c, at, :] = flat[c, at, :] * 0.5 if scale else zero
            return 0

        lax.fori_loop(0, ct, step, 0)

    @pl.when(tile > 0)
    def _():
        halo_row(0, True)

    @pl.when(tile == 0)
    def _():
        halo_row(0, False)

    @pl.when(tile < tiles_n - 1)
    def _():
        halo_row(1, True)

    @pl.when(tile == tiles_n - 1)
    def _():
        halo_row(1, False)

    def outer(i, _):
        shade_run(0, ct, i * (blocks - 1), 31)
        return 0

    lax.fori_loop(0, 2, outer, 0)

    wait_all(face.at[pl.ds(0, others)], f2_recv)

    def edge_planes(b, _):
        rs = pl.ds(pl.multiple_of(b * SUB, SUB), SUB)
        for side in range(2):
            p = side * (planes - 1)
            diffs = col_diffs([view(p, c, b, 0) for c in range(ct)], zero, zero, lane)
            for c in range(ct):
                other = face[c, side, rs, :]
                if side == 0:
                    plane_diff = view(1, c, b, 0) - other
                else:
                    plane_diff = other - view(planes - 2, c, b, 0)
                shaded[b, c, p] = shade(view(p, c, b, 1) - view(p, c, b, -1), plane_diff, diffs[c])
        return 0

    lax.fori_loop(0, blocks, edge_planes, 0)

    def by_segment(values):
        table = full(values[0])
        for s in range(1, len(values)):
            table = jnp.where(sub == s, values[s], table)
        return table

    knots = index.shape[0]
    points = [index[k].astype(jnp.float32) for k in range(knots)]
    lower = by_segment(points[:-1])
    upper = by_segment(points[1:])
    width = jnp.where(sub < knots - 1, upper - lower, 1.0)
    offsets, slopes = [], []
    for channel in range(4):
        scale = -LOG2E if channel == 0 else KC
        values = [
            extinct[k] if channel == 0 else color[channel - 1, k] for k in range(knots)
        ]
        begin, end = by_segment(values[:-1]), by_segment(values[1:])
        slope = (end - begin) / width
        offsets.append((begin - slope * lower) * scale)
        slopes.append(slope * scale)

    wait_all(part2.at[pl.ds(1, tiles_n - 1)], m2_recv)
    extremes = jnp.max(jnp.max(part2[...], axis=0), axis=1, keepdims=True)
    extremes = jnp.broadcast_to(extremes, (2, LANES))
    low_value = jnp.broadcast_to(-extremes[1:2, :], (SUB, LANES))
    span = jnp.broadcast_to(extremes[0:1, :] + extremes[1:2, :], (SUB, LANES)) + 0.5
    unit = span * (1.0 / (TABLE - 1.0))
    slopes = [slope * ((TABLE - 1.0) / span) for slope in slopes]
    bounds = [points[k] * unit for k in range(1, knots - 1)]
    odd = jnp.where(sub >= 6, BIG, jnp.where(sub >= 4, bounds[4], jnp.where(sub >= 2, bounds[2], bounds[0])))

    cores = 2
    chips = slabs // cores
    chip = me // cores
    mate = me + 1 - 2 * lax.rem(me, cores)
    pair = 2

    def render(owner, result):
        def rows_pair(i, _):
            def step(p, carry):
                out_carry = []
                for k in range(pair):
                    b = i * pair + k
                    through, sums = carry[k]
                    dist = view(p, owner, b, 0) - low_value
                    even = jnp.where(dist >= bounds[1], 2, 0)
                    even = jnp.where(dist >= bounds[3], 4, even)
                    even = jnp.where(dist >= bounds[5], 6, even)
                    segment = jnp.where(dist >= lookup(odd, even), even + 1, even)
                    offset = [lookup(t, segment) for t in offsets]
                    slope = [lookup(t, segment) for t in slopes]
                    rest = through * jnp.exp2(offset[0] + slope[0] * dist)
                    weight = (through - rest) * shaded[b, owner, p]
                    sums = tuple(
                        sums[n] + weight * (offset[n + 1] + slope[n + 1] * dist)
                        for n in range(3)
                    )
                    out_carry.append((rest, sums))
                return tuple(out_carry)

            begin = tuple((full(1.0), (full(0.0),) * 3) for _ in range(pair))
            done = lax.fori_loop(0, planes, step, begin, unroll=64)
            for k in range(pair):
                for n in range(3):
                    result[owner, i * pair + k, n] = done[k][1][n]
                result[owner, i * pair + k, 3] = done[k][0]
            return 0

        lax.fori_loop(0, blocks // pair, rows_pair, 0)

    def result_copy(owner):
        return pltpu.make_async_remote_copy(
            src_ref=packed.at[owner],
            dst_ref=gathered.at[me],
            send_sem=out_send,
            recv_sem=out_recv,
            device_id={"depth": owner},
            device_id_type=MESH,
        )

    def away(i, _):
        n = i // cores
        owner = cores * lax.rem(chip + 2 + (3 * n * n - 5 * n) // 2, chips) + i % cores
        render(owner, packed)
        result_copy(owner).start()
        return 0

    lax.fori_loop(0, slabs - cores, away, 0)
    render(mate, packed)
    result_copy(mate).start()
    render(me, gathered)

    @pl.when(tile < tiles_n - 1)
    def _():
        wait_all(volume.at[rows - 1], halo_send.at[0])

    @pl.when(tile > 0)
    def _():
        wait_all(volume.at[0], halo_send.at[1])

    wait_all(face_in.at[pl.ds(0, others)], f1_send)
    wait_all(face_out.at[pl.ds(0, others)], f2_send)
    wait_all(part1.at[pl.ds(1, others)], m1_send)
    wait_all(part2.at[pl.ds(1, tiles_n - 1)], m2_send)
    wait_all(packed.at[pl.ds(0, others)], out_send)

    wait_all(gathered.at[pl.ds(0, others)], out_recv)

    def composite(b, _):
        rs = pl.ds(pl.multiple_of(b * SUB, SUB), SUB)
        through = full(1.0)
        sums = [full(0.0)] * 3
        for p in range(slabs):
            slot = slots[p + 1]
            for i in range(3):
                sums[i] = sums[i] + through * gathered[slot, b, i]
            through = through * gathered[slot, b, 3]
        for i in range(3):
            out[i, rs, :] = sums[i]
        return 0

    lax.fori_loop(0, blocks, composite, 0)


def solution(mesh):
    tiles_n, slabs = mesh.shape["tile"], mesh.shape["depth"]

    def body(volume, slab_place, control_index, control_extinction, control_color):
        rows, planes, cols = volume.shape
        ct, blocks = cols // LANES, rows // SUB
        dims = (tiles_n, slabs, rows, planes, cols)
        f32, dma = jnp.float32, pltpu.SemaphoreType.DMA
        return pl.pallas_call(
            functools.partial(kernel, dims),
            out_shape=jax.ShapeDtypeStruct((3, rows, cols // slabs), f32),
            in_specs=[pl.BlockSpec(memory_space=pltpu.HBM)] * 5,
            out_specs=pl.BlockSpec(memory_space=pltpu.VMEM),
            scratch_shapes=[
                pltpu.VMEM((ct, rows, planes, LANES), f32),
                pltpu.VMEM((ct, planes + 1, rows + SUB, LANES), f32),
                pltpu.VMEM((blocks, ct, planes, SUB, LANES), f32),
                pltpu.VMEM((slabs + 1, 2, rows, LANES), f32),
                pltpu.VMEM((slabs, 2, rows, LANES), f32),
                pltpu.VMEM((slabs, 2, rows, LANES), f32),
                pltpu.VMEM((slabs, 2, LANES), f32),
                pltpu.VMEM((tiles_n, 2, LANES), f32),
                pltpu.VMEM((slabs, blocks, 4, SUB, LANES), f32),
                pltpu.VMEM((slabs, blocks, 4, SUB, LANES), f32),
                pltpu.SMEM(slab_place.shape, jnp.int32),
                pltpu.SMEM(control_index.shape, jnp.int32),
                pltpu.SMEM(control_extinction.shape, f32),
                pltpu.SMEM(control_color.shape, f32),
                pltpu.SMEM((slabs + 2,), jnp.int32),
                dma((4,)),
                dma((ct,)),
                dma((2,)),
                dma((2,)),
                *[dma(())] * 11,
            ],
            compiler_params=pltpu.CompilerParams(
                collective_id=0, has_side_effects=True, vmem_limit_bytes=48 << 20
            ),
            name="render",
        )(
            volume,
            *(
                pltpu.with_memory_space_constraint(x, pltpu.HBM)
                for x in (slab_place, control_index, control_extinction, control_color)
            ),
        )

    placed = (P("tile", "depth", None), P(), P(), P(), P())
    return jax.shard_map(
        body, mesh=mesh, in_specs=placed, out_specs=P(None, "tile", "depth"), check_vma=False
    )
```
